256 devices in a mesh: dp: 32 (over z_lo, x, core), shard: 8 (over z_hi, y).
Axes of the slice: x: 4, y: 4, z: 8 (z_hi: 2, z_lo: 4; z = z_hi * 4 + z_lo), core: 2. Of those that a mesh axis runs over, the one named last changes fastest.
Arguments:
- tokens: bfloat16 [32768, 1024], P(('dp', 'shard')), may hold values from -6 to 6
- cotangent: bfloat16 [32768, 1024], P(('dp', 'shard')), may hold values from -6 to 6
- assign: int32 [32768], P('dp'), may hold values from 0 to 1
- prob: float32 [32768], P('dp'), may hold values from 0.2 to 1
- w_gate: bfloat16 [2, 1024, 4096], P(None, None, 'shard'), may hold values from -0.1875 to 0.1875
- w_up: bfloat16 [2, 1024, 4096], P(None, None, 'shard'), may hold values from -0.1875 to 0.1875
- w_down: bfloat16 [2, 4096, 1024], P(None, 'shard'), may hold values from -0.09375 to 0.09375
Outputs:
- output: bfloat16 [32768, 1024], P(('dp', 'shard'))
- input_grad: bfloat16 [32768, 1024], P(('dp', 'shard'))
- grad_gate: float32 [2, 1024, 4096], P(None, 'dp', 'shard')
- grad_up: float32 [2, 1024, 4096], P(None, 'dp', 'shard')
- grad_down: float32 [2, 4096, 1024], P(None, 'shard', 'dp')
The draws below stay inside these ranges and needn't reach their ends.
All inputs are finite; a program needn't handle non-finite values.
Results may differ from the reference program's by a relative error of at most 0.0057.
Values may be sent and summed in bfloat16 or wider, within the bound.
No kernel may reach another device: no remote copies, remote signals or barrier semaphores. Data moves between devices by JAX's collectives and lax.ppermute only.
A program may use at most 128 MiB of HBM per device.

```python
import jax
import jax.numpy as jnp
from jax import lax

D = 1024
FF = 4096
EXP = 2
BLOCK = 128
TOKENS = 32768


def plant(values, rng, least, top_value):
    longest = values.shape.index(max(values.shape))
    spots = []
    for shift in (0, 1):
        where = [jax.random.randint(jax.random.fold_in(rng, axis), (), 0, length) for axis, length in enumerate(values.shape)]
        where[longest] = (where[longest] + shift) % values.shape[longest]
        spots.append(tuple(where))
    return values.at[spots[0]].set(least).at[spots[1]].set(top_value)


def levels(own_key, shape, shards, low, high):
    def one(axis_at, parts):
        steps = jax.random.uniform(jax.random.fold_in(jax.random.fold_in(own_key, 6), axis_at), (parts,), jnp.float32, low / len(shards), high / len(shards))
        return jnp.repeat(jnp.exp(steps), shape[axis_at] // parts).reshape((-1,) + (1,) * (len(shape) - axis_at - 1))

    gain = one(*shards[0])
    for cut in shards[1:]:
        gain = gain * one(*cut)
    return gain


def scatter_about(key, dims, scale, bound, pieces=(), kind=jnp.bfloat16):
    level = levels(key, dims, pieces, -0.22, 0.18) if pieces else 1.0
    array = jax.random.normal(key, dims, jnp.float32) * scale * level
    return jnp.minimum(jnp.maximum(array, -bound), bound).astype(kind)


def setup_inputs(seed: int = 0) -> dict:
    arg_keys = jax.random.split(jax.random.key(seed), 8)
    tokens = scatter_about(arg_keys[0], (TOKENS, D), 1.0, 6.0, ((0, 256),))
    cotangent = scatter_about(arg_keys[1], (TOKENS, D), 1.0, 6.0, ((0, 256),))
    assign = plant(jax.random.randint(arg_keys[2], (TOKENS,), 0, EXP), jax.random.fold_in(arg_keys[2], 1), 0, EXP - 1).astype(jnp.int32)
    prob = jnp.clip(0.2 + 0.8 * jax.random.uniform(arg_keys[3], (TOKENS,), jnp.float32) ** levels(arg_keys[3], (TOKENS,), ((0, 32),), -0.2, 0.2), 0.2, 1.0)
    w_gate = scatter_about(arg_keys[4], (EXP, D, FF), D ** -0.5, 0.1875, ((2, 8),))
    w_up = scatter_about(arg_keys[5], (EXP, D, FF), D ** -0.5, 0.1875, ((2, 8),))
    w_down = scatter_about(arg_keys[6], (EXP, FF, D), FF ** -0.5, 0.09375, ((1, 8),))
    return {"tokens": tokens, "cotangent": cotangent, "assign": assign, "prob": prob, "w_gate": w_gate, "w_up": w_up, "w_down": w_down}


def arrange(assign, experts, block_rows):
    row_count = assign.shape[0]
    labels = jnp.arange(experts, dtype=jnp.int32)
    onehot = (assign[:, None] == labels[None, :]).astype(jnp.int32)
    counts = jnp.sum(onehot, axis=0).astype(jnp.int32)
    blocks = ((counts + block_rows - 1) // block_rows).astype(jnp.int32)
    block_ends = jnp.cumsum(blocks).astype(jnp.int32)
    firsts = block_ends - blocks
    before = (jnp.cumsum(onehot, axis=0) - onehot).astype(jnp.int32)
    rank_in = jnp.sum(onehot * before, axis=1).astype(jnp.int32)
    token_slot = (jnp.sum(onehot * (firsts * block_rows)[None, :], axis=1) + rank_in).astype(jnp.int32)
    nblocks = row_count // block_rows + experts - 1
    slot_token = jnp.zeros((nblocks * block_rows,), jnp.int32).at[token_slot].set(jnp.arange(row_count, dtype=jnp.int32))
    slot_live = jnp.zeros((nblocks * block_rows,), jnp.float32).at[token_slot].set(1.0)
    block_index = jnp.arange(nblocks, dtype=jnp.int32)
    block_expert = jnp.minimum(jnp.sum((block_ends[None, :] <= block_index[:, None]).astype(jnp.int32), axis=1), experts - 1).astype(jnp.int32)
    return token_slot, slot_token, slot_live, block_expert


def add_at(total, expert, term):
    old = lax.dynamic_index_in_dim(total, expert, 0, keepdims=True)
    return lax.dynamic_update_index_in_dim(total, old + term[None], expert, 0)


def reference(tokens, cotangent, assign, prob, w_gate, w_up, w_down):
    token_slot, slot_token, slot_live, block_expert = arrange(assign, EXP, BLOCK)
    nblocks = block_expert.shape[0]
    scaled_grad = (prob[:, None] * cotangent.astype(jnp.float32)).astype(jnp.bfloat16)
    width = tokens.shape[1]

    def one_block(carry, block_index):
        grad_gate, grad_up, grad_down = carry
        chosen = lax.dynamic_slice_in_dim(slot_token, block_index * BLOCK, BLOCK)
        live = lax.dynamic_slice_in_dim(slot_live, block_index * BLOCK, BLOCK)
        expert = block_expert[block_index]
        gate_w = lax.dynamic_index_in_dim(w_gate, expert, 0, keepdims=False)
        up_w = lax.dynamic_index_in_dim(w_up, expert, 0, keepdims=False)
        down_w = lax.dynamic_index_in_dim(w_down, expert, 0, keepdims=False)
        rows_x = jnp.where(live[:, None] > 0, tokens[chosen], jnp.zeros((), tokens.dtype))
        rows_dout = jnp.where(live[:, None] > 0, scaled_grad[chosen], jnp.zeros((), scaled_grad.dtype))
        slot_prob = prob[chosen] * live
        gate_act = jnp.dot(rows_x, gate_w, preferred_element_type=jnp.float32)
        up_act = jnp.dot(rows_x, up_w, preferred_element_type=jnp.float32)
        sigma = jax.nn.sigmoid(gate_act)
        hidden = (gate_act * sigma * up_act).astype(jnp.bfloat16)
        partial_out = jnp.dot(hidden, down_w, preferred_element_type=jnp.float32)
        back_hidden = jnp.dot(rows_dout, down_w.T, preferred_element_type=jnp.float32)
        gate_grad = (back_hidden * up_act * sigma * (1.0 + gate_act * (1.0 - sigma))).astype(jnp.bfloat16)
        up_grad = (back_hidden * (gate_act * sigma)).astype(jnp.bfloat16)
        in_grad = jnp.dot(gate_grad, gate_w.T, preferred_element_type=jnp.float32) + jnp.dot(up_grad, up_w.T, preferred_element_type=jnp.float32)
        grad_gate = add_at(grad_gate, expert, jnp.dot(rows_x.T, gate_grad, preferred_element_type=jnp.float32))
        grad_up = add_at(grad_up, expert, jnp.dot(rows_x.T, up_grad, preferred_element_type=jnp.float32))
        grad_down = add_at(grad_down, expert, jnp.dot(hidden.T, rows_dout, preferred_element_type=jnp.float32))
        return (grad_gate, grad_up, grad_down), (slot_prob[:, None] * partial_out, in_grad)

    start = (jnp.zeros(w_gate.shape, jnp.float32), jnp.zeros(w_up.shape, jnp.float32), jnp.zeros(w_down.shape, jnp.float32))
    grads, stacked = lax.scan(one_block, start, jnp.arange(nblocks, dtype=jnp.int32))
    output = stacked[0].reshape(-1, width)[token_slot].astype(jnp.bfloat16)
    input_grad = stacked[1].reshape(-1, width)[token_slot].astype(jnp.bfloat16)
    return (output, input_grad, grads[0], grads[1], grads[2])
```

```python
import jax
import jax.numpy as jnp
from jax import lax
from jax.sharding import Mesh, PartitionSpec as P

EXP = 2
AXES = ("zlo", "x", "core", "zhi", "y")
SIZES = {"zlo": 4, "x": 4, "core": 2, "zhi": 2, "y": 4}
F32, BF16 = jnp.float32, jnp.bfloat16


def send(value, axis, step):
    n = SIZES[axis]
    return lax.ppermute(value, axis, [(i, (i + step) % n) for i in range(n)])


def relative(values):
    rows = values.shape[0] // 8
    blocks = values.reshape(2, 4, rows)[:, ::-1]
    doubled = jnp.tile(blocks, (2, 2, 1))
    start = (lax.axis_index("zhi"), 3 - lax.axis_index("y"), 0)
    return lax.dynamic_slice(doubled, start, (2, 4, rows)).reshape(-1)


def gather_group(block):
    far = send(block, "zhi", 1)
    parts = []
    for b in (block, far):
        parts += [b, send(b, "y", 1), send(b, "y", 2), send(b, "y", 3)]
    return jnp.concatenate(parts, axis=0)


def scatter_group(partial):
    width = partial.shape[1]
    p = partial.reshape(2, 4, -1, width)
    low = p.astype(BF16)
    total = p[:, 0]
    for k in (1, 2, 3):
        total = total + send(low[:, k], "y", -k).astype(F32)
    return total[0] + send(total[1].astype(BF16), "zhi", 1).astype(F32)


def scatter_rows(grad):
    e, d, f = grad.shape
    g = grad.reshape(e, 4, 4, 2, d // 32, f)
    for axis, at in (("core", 3), ("x", 2), ("zlo", 1)):
        n = SIZES[axis]
        me = lax.axis_index(axis)
        total = lax.dynamic_index_in_dim(g, me, at, keepdims=False)
        for k in range(1, n):
            piece = lax.dynamic_index_in_dim(g, (me + k) % n, at, keepdims=False)
            total = total + send(piece.astype(BF16), axis, k).astype(F32)
        g = total
    return g


def dot(a, b, ca, cb):
    return lax.dot_general(a, b, (((ca,), (cb,)), ((), ())), preferred_element_type=F32)


def per_device(tokens, cotangent, assign, prob, w_gate, w_up, w_down):
    rows, width = tokens.shape
    ff = w_gate.shape[2]
    x = gather_group(tokens)
    cot = gather_group(cotangent)
    second = relative(assign)[:, None] == 1
    scale = relative(prob)[:, None]
    zero = jnp.zeros((), BF16)

    def split(v):
        return jnp.concatenate([jnp.where(second, zero, v), jnp.where(second, v, zero)], axis=1)

    xx = split(x)
    gate_act = dot(xx, w_gate.reshape(EXP * width, ff), 1, 0)
    up_act = dot(xx, w_up.reshape(EXP * width, ff), 1, 0)
    sigma = jax.nn.sigmoid(gate_act)
    silu = gate_act * sigma
    hidden = (silu * up_act).astype(BF16)
    out_part = dot(split(hidden), w_down.reshape(EXP * ff, width), 1, 0)
    output = scatter_group(out_part) * scale[:rows]

    dout = (scale * cot.astype(F32)).astype(BF16)
    dd = split(dout)
    grad_down = dot(dd, hidden, 0, 0).reshape(EXP, width, ff)
    back = dot(dout, w_down.reshape(EXP * ff, width), 1, 1)
    back = jnp.where(second, back[:, ff:], back[:, :ff])
    gate_grad = (back * up_act * sigma * (1.0 + gate_act * (1.0 - sigma))).astype(BF16)
    up_grad = (back * silu).astype(BF16)
    grad_gate = dot(xx, gate_grad, 0, 0).reshape(EXP, width, ff)
    grad_up = dot(xx, up_grad, 0, 0).reshape(EXP, width, ff)
    gg, uu = split(gate_grad), split(up_grad)
    in_part = sum(
        dot(v[:, e * ff : (e + 1) * ff], w[e], 1, 1)
        for v, w in ((gg, w_gate), (uu, w_up))
        for e in range(EXP)
    )
    input_grad = scatter_group(in_part)
    return (
        output.astype(BF16),
        input_grad.astype(BF16),
        scatter_rows(grad_gate),
        scatter_rows(grad_up),
        scatter_rows(grad_down).swapaxes(1, 2),
    )


def solution(mesh):
    fine = Mesh(mesh.devices.reshape(*SIZES.values()), AXES)
    dp, shard = ("zlo", "x", "core"), ("zhi", "y")
    both = AXES
    return jax.shard_map(
        per_device,
        mesh=fine,
        in_specs=(
            P(both, None),
            P(both, None),
            P(dp),
            P(dp),
            P(None, None, shard),
            P(None, None, shard),
            P(None, shard, None),
        ),
        out_specs=(
            P(both, None),
            P(both, None),
            P(None, dp, shard),
            P(None, dp, shard),
            P(None, shard, dp),
        ),
        check_vma=False,
    )
```

```python
import jax
import jax.numpy as jnp
from jax import lax
from jax.experimental import pallas as pl
from jax.experimental.pallas import tpu as pltpu
from jax.sharding import Mesh, PartitionSpec as P

EXP = 2
AXES = ("zlo", "x", "core", "zhi", "y")
SIZES = {"zlo": 4, "x": 4, "core": 2, "zhi": 2, "y": 4}
F32, BF16 = jnp.float32, jnp.bfloat16
TILE = 256


def send(value, axis, step):
    n = SIZES[axis]
    return lax.ppermute(value, axis, [(i, (i + step) % n) for i in range(n)])


def relative(values):
    rows = values.shape[0] // 8
    blocks = values.reshape(2, 4, rows)[:, ::-1]
    doubled = jnp.tile(blocks, (2, 2, 1))
    start = (lax.axis_index("zhi"), 3 - lax.axis_index("y"), 0)
    return lax.dynamic_slice(doubled, start, (2, 4, rows)).reshape(-1, 1)


def gather_group(block):
    far = send(block, "zhi", 1)
    parts = []
    for b in (block, far):
        parts += [b, send(b, "y", 1), send(b, "y", 2), send(b, "y", 3)]
    return parts


def scatter_group(own, *pieces):
    total = own
    for k, piece in enumerate(pieces, 1):
        total = total + send(piece, "y", -k).astype(F32)
    return total[0] + send(total[1].astype(BF16), "zhi", 1).astype(F32)


def scatter_rows(own, other):
    total = own + send(other, "core", 1).astype(F32)
    for axis in ("x", "zlo"):
        g = total
        n = SIZES[axis]
        me = lax.axis_index(axis)
        total = lax.dynamic_index_in_dim(g, me, 0, keepdims=False)
        for k in range(1, n):
            piece = lax.dynamic_index_in_dim(g, (me + k) % n, 0, keepdims=False)
            total = total + send(piece.astype(BF16), axis, k).astype(F32)
    return total


def dot(a, b, ca, cb):
    return lax.dot_general(a, b, (((ca,), (cb,)), ((), ())), preferred_element_type=F32)


def split(value, second):
    zero = jnp.zeros_like(value)
    return jnp.where(second, zero, value), jnp.where(second, value, zero)


def put_rows(value, own, s1, s2, s3):
    i = pl.program_id(0)
    half = value.shape[0] // 2

    @pl.when(i % 2 == 0)
    def _():
        own[pl.ds(i // 2, 1)] = value[:half][None]
        s1[pl.ds(i // 2, 1)] = value[half:].astype(BF16)[None]

    @pl.when(i % 2 == 1)
    def _():
        s2[pl.ds(i // 2, 1)] = value[:half].astype(BF16)[None]
        s3[pl.ds(i // 2, 1)] = value[half:].astype(BF16)[None]


def put_grad(value, core, own, other):
    v = value.reshape(4, 2, value.shape[0] // 8, value.shape[1])
    first = core == 0
    own[...] = jnp.where(first, v[:, 0], v[:, 1])[:, None]
    other[...] = jnp.where(first, v[:, 1], v[:, 0]).astype(BF16)[:, None]


def forward_kernel(second_ref, *refs):
    blocks = refs[:8]
    wg, wu, wd, x_ref, hh_ref, a_ref, s_ref = refs[8:15]
    i = pl.program_id(0)
    n = blocks[0].shape[0]

    @pl.when(i == 0)
    def _():
        for b, block in enumerate(blocks):
            x_ref[b * n : (b + 1) * n] = block[...]

    rows = pl.ds(pl.multiple_of(i * TILE, TILE), TILE)
    second = second_ref[rows] > 0
    x0, x1 = split(x_ref[rows], second)
    xx = jnp.concatenate([x0, x1], axis=1)
    gate = dot(xx, wg[...], 1, 0)
    up = dot(xx, wu[...], 1, 0)
    sigma = 1.0 / (1.0 + jnp.exp(-gate))
    silu = gate * sigma
    a_ref[...] = up * sigma * (1.0 + gate * (1.0 - sigma))
    s_ref[...] = silu
    hidden = (silu * up).astype(BF16)
    hh = jnp.concatenate(split(hidden, second), axis=1)
    hh_ref[...] = hh
    put_rows(dot(hh, wd[...], 1, 0), *refs[15:19])


def down_kernel(core_ref, scale_ref, *refs):
    blocks = refs[:8]
    hh, dout, own, other = refs[8:]
    i = pl.program_id(0)
    n = blocks[0].shape[0]

    @pl.when(i == 0)
    def _():
        for b, block in enumerate(blocks):
            at = slice(b * n, (b + 1) * n)
            dout[at] = (scale_ref[at] * block[...].astype(F32)).astype(BF16)

    columns = pl.ds(pl.multiple_of(i * TILE, TILE), TILE)
    put_grad(dot(dout[:, columns], hh[...], 0, 0), core_ref[0], own, other)


def back_kernel(second_ref, dout, wd, a_ref, s_ref, gu_ref):
    second = second_ref[...] > 0
    ff = a_ref.shape[1]
    both = dot(dout[...], wd[...], 1, 1)
    back = jnp.where(second, both[:, ff:], both[:, :ff])
    gate_grad = (back * a_ref[...]).astype(BF16)
    up_grad = (back * s_ref[...]).astype(BF16)
    gu_ref[...] = jnp.concatenate(split(gate_grad, second) + split(up_grad, second), axis=1)


def weight_kernel(core_ref, x_ref, gu, own, other):
    put_grad(dot(x_ref[...], gu[...], 0, 0), core_ref[0], own, other)


def input_kernel(gu, wg, wu, *outs):
    ff = wg.shape[2]
    total = None
    for j, w in enumerate((wg, wu)):
        for e in range(EXP):
            c = (j * EXP + e) * ff
            term = dot(gu[:, c : c + ff], w[e], 1, 1)
            total = term if total is None else total + term
    put_rows(total, *outs)


def call(kernel, grid, ins, outs, flops, scalars=0):
    moved = sum(a.size * a.dtype.itemsize for *_, a in ins + outs)
    return pl.pallas_call(
        kernel,
        out_shape=[jax.ShapeDtypeStruct(a.shape, a.dtype) for *_, a in outs],
        grid_spec=pltpu.PrefetchScalarGridSpec(
            num_scalar_prefetch=scalars,
            grid=(grid,),
            in_specs=[pl.BlockSpec(b, m) for b, m, _ in ins],
            out_specs=[pl.BlockSpec(b, m) for b, m, _ in outs],
        ),
        compiler_params=pltpu.CompilerParams(vmem_limit_bytes=56 << 20),
        cost_estimate=pl.CostEstimate(flops=flops, bytes_accessed=moved, transcendentals=0),
    )


def whole(a):
    return (a.shape, lambda i, *_: (0,) * len(a.shape), a)


def tiled(a, axis, size):
    block = tuple(size if d == axis else n for d, n in enumerate(a.shape))
    return (block, lambda i, *_: tuple(i if d == axis else 0 for d in range(len(a.shape))), a)


def sds(shape, dtype):
    return jax.ShapeDtypeStruct(shape, dtype)


def per_device(tokens, cotangent, assign, prob, w_gate, w_up, w_down):
    block, width = tokens.shape
    rows = assign.shape[0]
    ff = w_gate.shape[2]
    steps = rows // TILE
    own_rows = width // 32
    wide = EXP * ff
    unit = 2 * rows * width * ff * EXP
    second = relative(assign)
    scale = relative(prob)
    core = lax.axis_index("core").astype(jnp.int32).reshape(1)
    xs = gather_group(tokens)
    ds = gather_group(cotangent)
    wg2, wu2 = (w.reshape(EXP * width, ff) for w in (w_gate, w_up))
    wd2 = w_down.reshape(wide, width)
    pieces = [whole(sds((2, block, width), t)) for t in (F32, BF16, BF16, BF16)]

    def grads(columns):
        return [tiled(sds((4, 4, own_rows, columns), t), 1, 1) for t in (F32, BF16)]

    ins = [whole(a) for a in (second, *xs, wg2, wu2, wd2)]
    outs = [
        whole(sds((rows, width), BF16)),
        tiled(sds((rows, wide), BF16), 0, TILE),
        tiled(sds((rows, ff), F32), 0, TILE),
        tiled(sds((rows, ff), F32), 0, TILE),
        *pieces,
    ]
    x, hh, act, silu, *out_pieces = call(forward_kernel, steps, ins, outs, 3 * unit)(*(a for *_, a in ins))

    ins = [whole(a) for a in (scale, *ds, hh)]
    outs = [whole(sds((rows, width), BF16)), *grads(wide)]
    dout, *down = call(down_kernel, 4, ins, outs, unit, 1)(core, *(a for *_, a in ins))

    ins = [tiled(second, 0, TILE), tiled(dout, 0, TILE), whole(wd2), tiled(act, 0, TILE), tiled(silu, 0, TILE)]
    outs = [tiled(sds((rows, 2 * wide), BF16), 0, TILE)]
    (gu,) = call(back_kernel, steps, ins, outs, unit)(*(a for *_, a in ins))

    ins = [tiled(x, 1, TILE), whole(gu)]
    gate_up = call(weight_kernel, 4, ins, grads(2 * wide), 2 * unit, 1)(core, *(a for *_, a in ins))

    gu, gate_up = lax.optimization_barrier((gu, gate_up))
    ins = [tiled(gu, 0, TILE), whole(w_gate), whole(w_up)]
    in_pieces = call(input_kernel, steps, ins, pieces, 2 * unit)(*(a for *_, a in ins))

    output = scatter_group(*out_pieces) * scale[:block]
    grad_down = scatter_rows(*down).reshape(own_rows, EXP, ff)
    both = scatter_rows(*gate_up).reshape(own_rows, 2, EXP, ff)
    input_grad = scatter_group(*in_pieces)
    return (
        output.astype(BF16),
        input_grad.astype(BF16),
        both[:, 0].swapaxes(0, 1),
        both[:, 1].swapaxes(0, 1),
        grad_down.transpose(1, 2, 0),
    )


def solution(mesh):
    fine = Mesh(mesh.devices.reshape(*SIZES.values()), AXES)
    dp, shard = ("zlo", "x", "core"), ("zhi", "y")
    return jax.shard_map(
        per_device,
        mesh=fine,
        in_specs=(
            P(AXES, None),
            P(AXES, None),
            P(dp),
            P(dp),
            P(None, None, shard),
            P(None, None, shard),
            P(None, shard, None),
        ),
        out_specs=(
            P(AXES, None),
            P(AXES, None),
            P(None, dp, shard),
            P(None, dp, shard),
            P(None, shard, dp),
        ),
        check_vma=False,
    )
```

```python
import jax
import jax.numpy as jnp
from jax import lax
from jax.experimental import pallas as pl
from jax.experimental.pallas import tpu as pltpu
from jax.sharding import Mesh, PartitionSpec as P

EXP = 2
AXES = ("zlo", "x", "core", "zhi", "y")
SIZES = {"zlo": 4, "x": 4, "core": 2, "zhi": 2, "y": 4}
F32, BF16 = jnp.float32, jnp.bfloat16
TILE = 256
PARTS = 5


def send(value, axis, step):
    n = SIZES[axis]
    return lax.ppermute(value, axis, [(i, (i + step) % n) for i in range(n)])


def relative(values):
    rows = values.shape[0] // 8
    blocks = values.reshape(2, 4, rows)[:, ::-1]
    doubled = jnp.tile(blocks, (2, 2, 1))
    start = (lax.axis_index("zhi"), 3 - lax.axis_index("y"), 0)
    return lax.dynamic_slice(doubled, start, (2, 4, rows)).reshape(-1, 1)


def after(value, *first):
    return lax.optimization_barrier((value, first))[0]


def pass_on(left, right):
    half = left.shape[0] // 2
    return send(left[:half], "y", 1), send(right[half:], "y", -1)


def pick(total, axis):
    n = SIZES[axis]
    me = lax.axis_index(axis)
    own = lax.dynamic_index_in_dim(total, me, 0, keepdims=False)
    return own, [lax.dynamic_index_in_dim(total, (me + k) % n, 0, keepdims=False).astype(BF16) for k in range(1, n)]


def sends(pieces, axis, way=1):
    return [send(piece, axis, way * k) for k, piece in enumerate(pieces, 1)]


def add(own, pieces):
    for piece in pieces:
        own = own + piece.astype(F32)
    return own


def dot(a, b, ca, cb):
    return lax.dot_general(a, b, (((ca,), (cb,)), ((), ())), preferred_element_type=F32)


def split(value, second):
    zero = jnp.zeros_like(value)
    return jnp.where(second, zero, value), jnp.where(second, value, zero)


def put_rows(value, own, s1, s2, s3):
    i = pl.program_id(0)
    half = value.shape[0] // 2

    @pl.when(i == 0)
    def _():
        own[...] = value[:half]
        s1[...] = value[half:].astype(BF16)

    @pl.when(i == 1)
    def _():
        s2[...] = value[:half].astype(BF16)
        s3[...] = value[half:].astype(BF16)


def put_grad(value, core, own, other):
    v = value.reshape(4, 2, value.shape[0] // 8, value.shape[1])
    first = core == 0
    own[...] = jnp.where(first, v[:, 0], v[:, 1])[:, None]
    other[...] = jnp.where(first, v[:, 1], v[:, 0]).astype(BF16)[:, None]


def join(blocks, out, scale=None):
    at = 0
    for block in blocks:
        rows = slice(at, at + block.shape[0])
        value = block[...]
        out[rows] = value if scale is None else (scale[rows] * value.astype(F32)).astype(BF16)
        at = rows.stop


def forward_kernel(second_ref, *refs):
    wg, wu, wd, x_ref, hh_ref, a_ref, s_ref = refs[PARTS : PARTS + 7]
    i = pl.program_id(0)

    @pl.when(i == 0)
    def _():
        join(refs[:PARTS], x_ref)

    rows = pl.ds(pl.multiple_of(i * TILE, TILE), TILE)
    second = second_ref[rows] > 0
    xx = jnp.concatenate(split(x_ref[rows], second), axis=1)
    gate = dot(xx, wg[...], 1, 0)
    up = dot(xx, wu[...], 1, 0)
    sigma = 1.0 / (1.0 + jnp.exp(-gate))
    silu = gate * sigma
    a_ref[...] = up * sigma * (1.0 + gate * (1.0 - sigma))
    s_ref[...] = silu
    hidden = (silu * up).astype(BF16)
    hh = jnp.concatenate(split(hidden, second), axis=1)
    hh_ref[...] = hh
    put_rows(dot(hh, wd[...], 1, 0), *refs[PARTS + 7 :])


def back_kernel(second_ref, scale_ref, *refs):
    a_ref, s_ref, wd, dout, gu_ref = refs[PARTS:]
    i = pl.program_id(0)

    @pl.when(i == 0)
    def _():
        join(refs[:PARTS], dout, scale_ref)

    rows = pl.ds(pl.multiple_of(i * TILE, TILE), TILE)
    second = second_ref[rows] > 0
    ff = a_ref.shape[1]
    both = dot(dout[rows], wd[...], 1, 1)
    back = jnp.where(second, both[:, ff:], both[:, :ff])
    gate_grad = (back * a_ref[...]).astype(BF16)
    up_grad = (back * s_ref[...]).astype(BF16)
    gu_ref[...] = jnp.concatenate(split(gate_grad, second) + split(up_grad, second), axis=1)


def outer_kernel(core_ref, left0, left1, right0, right1, own, other):
    total = dot(left0[...], right0[...], 0, 0) + dot(left1[...], right1[...], 0, 0)
    put_grad(total, core_ref[0], own, other)


def input_kernel(gu, wg, wu, *outs):
    ff = wg.shape[2]
    total = None
    for j, w in enumerate((wg, wu)):
        for e in range(EXP):
            c = (j * EXP + e) * ff
            term = dot(gu[:, c : c + ff], w[e], 1, 1)
            total = term if total is None else total + term
    put_rows(total, *outs)


def call(kernel, grid, ins, outs, flops, scalars=0):
    moved = sum(a.size * a.dtype.itemsize for *_, a in ins + outs)
    return pl.pallas_call(
        kernel,
        out_shape=[jax.ShapeDtypeStruct(a.shape, a.dtype) for *_, a in outs],
        grid_spec=pltpu.PrefetchScalarGridSpec(
            num_scalar_prefetch=scalars,
            grid=(grid,),
            in_specs=[pl.BlockSpec(b, m) for b, m, _ in ins],
            out_specs=[pl.BlockSpec(b, m) for b, m, _ in outs],
        ),
        compiler_params=pltpu.CompilerParams(vmem_limit_bytes=56 << 20),
        cost_estimate=pl.CostEstimate(flops=flops // 40, bytes_accessed=moved // 40, transcendentals=0),
    )


def whole(a):
    return (a.shape, lambda i, *_: (0,) * len(a.shape), a)


def tiled(a, axis, size):
    block = tuple(size if d == axis else n for d, n in enumerate(a.shape))
    return (block, lambda i, *_: tuple(i if d == axis else 0 for d in range(len(a.shape))), a)


def sds(shape, dtype):
    return jax.ShapeDtypeStruct(shape, dtype)


def per_device(tokens, cotangent, assign, prob, w_gate, w_up, w_down):
    block, width = tokens.shape
    rows = assign.shape[0] // 2
    ff = w_gate.shape[2]
    steps = rows // TILE
    own_rows = width // 32
    wide = EXP * ff
    unit = 2 * rows * width * ff * EXP
    second = relative(assign)
    scale = relative(prob)
    core = lax.axis_index("core").astype(jnp.int32).reshape(1)
    wg2, wu2 = (w.reshape(EXP * width, ff) for w in (w_gate, w_up))
    wd2 = w_down.reshape(wide, width)

    t1, t3 = send(tokens, "y", 1), send(tokens, "y", -1)
    tz = send(tokens, "zhi", 1)
    t2 = pass_on(t1, t3)
    cot = after(cotangent, t1, t3)
    c1, c3 = send(cot, "y", 1), send(cot, "y", -1)
    u1, u3 = send(tz, "y", 1), send(tz, "y", -1)
    cz = send(after(cotangent, tz), "zhi", 1)
    u2 = pass_on(u1, u3)
    c2 = pass_on(c1, c3)
    d1, d3 = send(cz, "y", 1), send(cz, "y", -1)
    d2 = pass_on(d1, d3)
    xs = ((tokens, t1, *t2, t3), (tz, u1, *u2, u3))
    ds = ((cotangent, c1, *c2, c3), (cz, d1, *d2, d3))

    pieces = [whole(sds((block, width), t)) for t in (F32, BF16, BF16, BF16)]

    def grads(columns):
        return [tiled(sds((4, 4, own_rows, columns), t), 1, 1) for t in (F32, BF16)]

    def run(kernel, steps, ins, outs, flops, *scalars):
        return call(kernel, steps, ins, outs, flops, len(scalars))(*scalars, *(a for *_, a in ins))

    def forward(h, blocks):
        ins = [whole(a) for a in (second[h * rows : (h + 1) * rows], *blocks, wg2, wu2, wd2)]
        outs = [
            whole(sds((rows, width), BF16)),
            tiled(sds((rows, wide), BF16), 0, TILE),
            tiled(sds((rows, ff), F32), 0, TILE),
            tiled(sds((rows, ff), F32), 0, TILE),
            *pieces,
        ]
        return run(forward_kernel, steps, ins, outs, 3 * unit)

    def backward(h, blocks, act, silu):
        at = slice(h * rows, (h + 1) * rows)
        ins = [whole(a) for a in (second[at], scale[at], *blocks)]
        ins += [tiled(act, 0, TILE), tiled(silu, 0, TILE), whole(wd2)]
        outs = [whole(sds((rows, width), BF16)), tiled(sds((rows, 2 * wide), BF16), 0, TILE)]
        return run(back_kernel, steps, ins, outs, unit)

    def outer(left, right, part=0):
        columns = ((rows, wide), lambda i, *_: (0, part))
        ins = [*(tiled(a, 1, TILE) for a in left), *((*columns, a) for a in right)]
        return run(outer_kernel, 4, ins, grads(wide), unit, core)

    def inputs(gu):
        ins = [tiled(gu, 0, TILE), whole(w_gate), whole(w_up)]
        return run(input_kernel, steps, ins, pieces, 2 * unit)

    x0, hh0, act0, silu0, *out0 = forward(0, xs[0])
    out0_y = sends(out0[1:], "y", -1)
    x1, hh1, act1, silu1, *out1 = forward(1, after(xs[1], hh0))
    out1_y = sends(out1[1:], "y", -1)
    dout0, gu0 = backward(0, after(ds[0], x1), act0, silu0)
    dout1, gu1 = backward(1, after(ds[1], gu0), act1, silu1)
    far = add(out1[0], after(out1_y, gu1)).astype(BF16)
    down, other = outer(after((dout0, dout1), far), (hh0, hh1))
    down_c = send(other, "core", 1)
    far_z = send(far, "zhi", 1)
    in1 = inputs(after(gu1, down))
    in1_y = sends(in1[1:], "y", -1)
    near = add(out0[0], after([*out0_y, far_z], in1))
    output = (near * scale[:block]).astype(BF16)
    down, down_x = pick(add(down, after([down_c], output)), "x")
    gate, other = outer(after((x0, x1), down, down_x), (gu0, gu1), 0)
    down_x = sends(down_x, "x")
    gate_c = send(other, "core", 1)
    up, other = outer(after((x0, x1), gate), (gu0, gu1), 1)
    up_c = send(other, "core", 1)
    far = add(in1[0], after(in1_y, up)).astype(BF16)
    gate, gate_x = pick(add(gate, after([gate_c], far)), "x")
    in0 = inputs(after(gu0, gate, gate_x))
    gate_x = sends(gate_x, "x")
    far_z = send(far, "zhi", 1)
    in0_y = sends(in0[1:], "y", -1)
    up, up_x = pick(add(up, after([up_c], in0)), "x")
    up_x = sends(up_x, "x")
    down = add(down, after(down_x, up))
    gate = add(gate, after(gate_x, up))
    pair, pair_z = pick(jnp.concatenate([down, gate], axis=2), "zlo")
    near = add(in0[0], after([*in0_y, far_z], pair, pair_z))
    pair_z = sends(pair_z, "zlo")
    input_grad = near.astype(BF16)
    up, up_z = pick(add(up, after(up_x, input_grad)), "zlo")
    up_z = sends(up_z, "zlo")
    pair = add(pair, after(pair_z, up_z)).reshape(own_rows, 2, EXP, ff)
    up = add(up, up_z).reshape(own_rows, EXP, ff)
    return (
        output,
        input_grad,
        pair[:, 1].swapaxes(0, 1),
        up.swapaxes(0, 1),
        pair[:, 0].transpose(1, 2, 0),
    )


def solution(mesh):
    fine = Mesh(mesh.devices.reshape(*SIZES.values()), AXES)
    dp, shard = ("zlo", "x", "core"), ("zhi", "y")
    return jax.shard_map(
        per_device,
        mesh=fine,
        in_specs=(
            P(AXES, None),
            P(AXES, None),
            P(dp),
            P(dp),
            P(None, None, shard),
            P(None, None, shard),
            P(None, shard, None),
        ),
        out_specs=(
            P(AXES, None),
            P(AXES, None),
            P(None, dp, shard),
            P(None, dp, shard),
            P(None, shard, dp),
        ),
        check_vma=False,
    )
```

```python
import jax
import jax.numpy as jnp
from jax import lax
from jax.experimental import pallas as pl
from jax.experimental.pallas import tpu as pltpu
from jax.sharding import Mesh, PartitionSpec as P

EXP = 2
AXES = ("zlo", "x", "core", "zhi", "y")
SIZES = {"zlo": 4, "x": 4, "core": 2, "zhi": 2, "y": 4}
F32, BF16 = jnp.float32, jnp.bfloat16
TILE = 256


def send(value, axis, step):
    n = SIZES[axis]
    return lax.ppermute(value, axis, [(i, (i + step) % n) for i in range(n)])


def after(value, *first):
    return lax.optimization_barrier((value, first))[0]


def exchange(value, axis):
    return lax.all_to_all(value, axis, 0, 0, tiled=True)


def near_first(values):
    v = values.reshape(2, -1)
    return jnp.where(lax.axis_index("zhi") == 0, v, v[::-1]).reshape(-1, 1)


def gather_y(block):
    copies = jnp.broadcast_to(block[None], (SIZES["y"], *block.shape))
    return exchange(copies, "y").reshape(-1, block.shape[-1])


def total(pieces):
    value = pieces[0].astype(F32)
    for k in range(1, pieces.shape[0]):
        value = value + pieces[k].astype(F32)
    return value


def pick(value, axis):
    n = SIZES[axis]
    me = lax.axis_index(axis)
    own = lax.dynamic_index_in_dim(value, me, 0, keepdims=False)
    return own, [lax.dynamic_index_in_dim(value, (me + k) % n, 0, keepdims=False).astype(BF16) for k in range(1, n)]


def add(own, pieces, axis):
    for k, piece in enumerate(pieces, 1):
        own = own + send(piece, axis, k).astype(F32)
    return own


def dot(a, b, ca, cb):
    return lax.dot_general(a, b, (((ca,), (cb,)), ((), ())), preferred_element_type=F32)


def split(value, second):
    zero = jnp.zeros_like(value)
    return jnp.where(second, zero, value), jnp.where(second, value, zero)


def put_grad(value, core, own, other):
    v = value.reshape(4, 2, value.shape[0] // 8, value.shape[1])
    first = core == 0
    own[...] = jnp.where(first, v[:, 0], v[:, 1])[:, None]
    other[...] = jnp.where(first, v[:, 1], v[:, 0]).astype(BF16)[:, None]


def forward_kernel(second_ref, near, far, wg, wu, wd, hh_ref, a_ref, s_ref, out_ref):
    second = second_ref[...] > 0
    x = jnp.where(pl.program_id(0) < 2, near[...], far[...])
    xx = jnp.concatenate(split(x, second), axis=1)
    gate = dot(xx, wg[...], 1, 0)
    up = dot(xx, wu[...], 1, 0)
    sigma = 1.0 / (1.0 + jnp.exp(-gate))
    silu = gate * sigma
    a_ref[...] = up * sigma * (1.0 + gate * (1.0 - sigma))
    s_ref[...] = silu
    hidden = (silu * up).astype(BF16)
    hh = jnp.concatenate(split(hidden, second), axis=1)
    hh_ref[...] = hh
    out_ref[...] = dot(hh, wd[...], 1, 0).astype(BF16).reshape(out_ref.shape)


def down_kernel(core_ref, scale_ref, near, far, hh, dout, own, other):
    i = pl.program_id(0)
    rows = near.shape[0]

    @pl.when(i == 0)
    def _():
        for h, block in enumerate((near, far)):
            at = slice(h * rows, (h + 1) * rows)
            dout[at] = (scale_ref[at] * block[...].astype(F32)).astype(BF16)

    columns = pl.ds(pl.multiple_of(i * TILE, TILE), TILE)
    put_grad(dot(dout[:, columns], hh[...], 0, 0), core_ref[0], own, other)


def back_kernel(second_ref, dout, wd, a_ref, s_ref, gu_ref):
    second = second_ref[...] > 0
    ff = a_ref.shape[1]
    both = dot(dout[...], wd[...], 1, 1)
    back = jnp.where(second, both[:, ff:], both[:, :ff])
    gate_grad = (back * a_ref[...]).astype(BF16)
    up_grad = (back * s_ref[...]).astype(BF16)
    gu_ref[...] = jnp.concatenate(split(gate_grad, second) + split(up_grad, second), axis=1)


def weight_kernel(core_ref, near, far, gu, own, other):
    rows = near.shape[0]
    value = dot(near[...], gu[:rows], 0, 0) + dot(far[...], gu[rows:], 0, 0)
    put_grad(value, core_ref[0], own, other)


def input_kernel(gu, wg, wu, near, far):
    ff = wg.shape[2]
    i = pl.program_id(0)
    value = None
    for j, w in enumerate((wg, wu)):
        for e in range(EXP):
            c = (j * EXP + e) * ff
            term = dot(gu[:, c : c + ff], w[e], 1, 1)
            value = term if value is None else value + term
    value = value.astype(BF16).reshape(2, -1, value.shape[1])

    @pl.when(i < 2)
    def _():
        near[pl.ds(2 * i, 2)] = value

    @pl.when(i >= 2)
    def _():
        far[pl.ds(2 * i - 4, 2)] = value


def call(kernel, grid, ins, outs, flops, scalars=0):
    moved = sum(a.size * a.dtype.itemsize for *_, a in ins + outs)
    return pl.pallas_call(
        kernel,
        out_shape=[jax.ShapeDtypeStruct(a.shape, a.dtype) for *_, a in outs],
        grid_spec=pltpu.PrefetchScalarGridSpec(
            num_scalar_prefetch=scalars,
            grid=(grid,),
            in_specs=[pl.BlockSpec(b, m) for b, m, _ in ins],
            out_specs=[pl.BlockSpec(b, m) for b, m, _ in outs],
        ),
        compiler_params=pltpu.CompilerParams(vmem_limit_bytes=56 << 20),
        cost_estimate=pl.CostEstimate(flops=flops, bytes_accessed=moved, transcendentals=0),
    )


def whole(a):
    return (a.shape, lambda i, *_: (0,) * len(a.shape), a)


def tiled(a, axis, size):
    block = tuple(size if d == axis else n for d, n in enumerate(a.shape))
    return (block, lambda i, *_: tuple(i if d == axis else 0 for d in range(len(a.shape))), a)


def sds(shape, dtype):
    return jax.ShapeDtypeStruct(shape, dtype)


def per_device(tokens, cotangent, assign, prob, w_gate, w_up, w_down):
    block, width = tokens.shape
    rows = assign.shape[0]
    ff = w_gate.shape[2]
    own_rows = width // 32
    wide = EXP * ff
    unit = 2 * rows * width * ff * EXP
    second = near_first(assign)
    scale = near_first(prob)
    core = lax.axis_index("core").astype(jnp.int32).reshape(1)
    wg2, wu2 = (w.reshape(EXP * width, ff) for w in (w_gate, w_up))
    wd2 = w_down.reshape(wide, width)
    half = rows // 2

    def pieces_of(columns):
        return [tiled(sds((4, 4, own_rows, columns), t), 1, 1) for t in (F32, BF16)]

    def run(kernel, ins, outs, flops, *scalars):
        return call(kernel, 4, ins, outs, flops, len(scalars))(*scalars, *(a for *_, a in ins))

    far_tokens = send(tokens, "zhi", 1)
    x0 = gather_y(tokens)
    x1 = gather_y(far_tokens)
    far_cot = send(after(cotangent, far_tokens), "zhi", 1)
    d0 = gather_y(after(cotangent, x0))
    d1 = gather_y(after(far_cot, x1))

    tile = (TILE, width)
    ins = [tiled(second, 0, TILE)]
    ins += [(tile, lambda i: (jnp.minimum(i, 1), 0), x0), (tile, lambda i: (jnp.maximum(i - 2, 0), 0), x1)]
    ins += [whole(a) for a in (wg2, wu2, wd2)]
    outs = [tiled(sds((rows, wide), BF16), 0, TILE)]
    outs += [tiled(sds((rows, ff), F32), 0, TILE)] * 2
    outs += [((2, 1, block, width), lambda i: (i % 2, i // 2, 0, 0), sds((4, 2, block, width), BF16))]
    hh, act, silu, out = run(forward_kernel, ins, outs, 3 * unit)
    out = exchange(out, "y")

    ins = [whole(a) for a in (scale, d0, d1, hh)]
    outs = [whole(sds((rows, width), BF16)), *pieces_of(wide)]
    dout, down, other = run(down_kernel, ins, outs, unit, core)
    down_c = send(other, "core", 1)

    ins = [tiled(after(second, down), 0, TILE), tiled(dout, 0, TILE), whole(wd2), tiled(act, 0, TILE), tiled(silu, 0, TILE)]
    (gu,) = run(back_kernel, ins, [tiled(sds((rows, 2 * wide), BF16), 0, TILE)], unit)

    out = total(after(out, gu))
    far_out = send(out[1].astype(BF16), "zhi", 1)
    down = (down + after(down_c, gu).astype(F32)).astype(BF16)

    x0, x1 = after((x0, x1), down, out)
    ins = [tiled(x0, 1, TILE), tiled(x1, 1, TILE), whole(gu)]
    both, other = run(weight_kernel, ins, pieces_of(2 * wide), 2 * unit, core)
    down = exchange(down, "x")
    both_c = send(other, "core", 1)

    own_scale = lax.dynamic_slice_in_dim(scale, lax.axis_index("y") * block, block)
    output = ((out[0] + after(far_out, both).astype(F32)) * own_scale).astype(BF16)
    ins = [tiled(after(gu, both, output), 0, TILE), whole(w_gate), whole(w_up)]
    outs = [whole(sds((4, block, width), BF16))] * 2
    near, far = run(input_kernel, ins, outs, 2 * unit)

    both, pieces = pick(both + after(both_c, near).astype(F32), "x")
    far, near, both = after((far, near, both), pieces)
    both = add(both, pieces, "x")
    far = exchange(far, "y")
    near = exchange(after(near, far), "y")
    far = send(total(far).astype(BF16), "zhi", 1)
    grads = jnp.concatenate([total(down), both], axis=2).astype(BF16)
    grads = exchange(after(grads, near), "zlo")
    input_grad = (total(near) + far.astype(F32)).astype(BF16)
    grads = total(grads).reshape(own_rows, 3, EXP, ff)
    return (
        output,
        input_grad,
        grads[:, 1].swapaxes(0, 1),
        grads[:, 2].swapaxes(0, 1),
        grads[:, 0].transpose(1, 2, 0),
    )


def solution(mesh):
    fine = Mesh(mesh.devices.reshape(*SIZES.values()), AXES)
    dp, shard = ("zlo", "x", "core"), ("zhi", "y")
    return jax.shard_map(
        per_device,
        mesh=fine,
        in_specs=(
            P(AXES, None),
            P(AXES, None),
            P(dp),
            P(dp),
            P(None, None, shard),
            P(None, None, shard),
            P(None, shard, None),
        ),
        out_specs=(
            P(AXES, None),
            P(AXES, None),
            P(None, dp, shard),
            P(None, dp, shard),
            P(None, shard, dp),
        ),
        check_vma=False,
    )
```

```python
import jax
import jax.numpy as jnp
from jax import lax
from jax.experimental import pallas as pl
from jax.experimental.pallas import tpu as pltpu
from jax.sharding import Mesh, PartitionSpec as P

EXP = 2
AXES = ("zlo", "x", "core", "zhi", "y")
SIZES = {"zlo": 4, "x": 4, "core": 2, "zhi": 2, "y": 4}
F32, BF16 = jnp.float32, jnp.bfloat16
TILE = 256


def send(value, axis, step):
    n = SIZES[axis]
    return lax.ppermute(value, axis, [(i, (i + step) % n) for i in range(n)])


def tie(*values):
    return lax.optimization_barrier(values)


def exchange(value, axis):
    return lax.all_to_all(value, axis, 0, 0, tiled=True)


def near_first(values):
    v = values.reshape(2, -1)
    return jnp.where(lax.axis_index("zhi") == 0, v, v[::-1]).reshape(-1, 1)


def gather_y(block):
    copies = jnp.broadcast_to(block[None], (SIZES["y"], *block.shape))
    return exchange(copies, "y").reshape(-1, block.shape[-1])


def total(pieces):
    value = pieces[0].astype(F32)
    for k in range(1, pieces.shape[0]):
        value = value + pieces[k].astype(F32)
    return value


def pick(value, axis):
    n = SIZES[axis]
    me = lax.axis_index(axis)
    own = lax.dynamic_index_in_dim(value, me, 0, keepdims=False)
    return own, [lax.dynamic_index_in_dim(value, (me + k) % n, 0, keepdims=False).astype(BF16) for k in range(1, n)]


def sends(pieces, axis):
    return [send(piece, axis, k) for k, piece in enumerate(pieces, 1)]


def add(own, pieces):
    for piece in pieces:
        own = own + piece.astype(F32)
    return own


def dot(a, b, ca, cb):
    return lax.dot_general(a, b, (((ca,), (cb,)), ((), ())), preferred_element_type=F32)


def split(value, second):
    zero = jnp.zeros_like(value)
    return jnp.where(second, zero, value), jnp.where(second, value, zero)


def put_grad(value, core, own, other):
    v = value.reshape(4, 2, value.shape[0] // 8, value.shape[1])
    first = core == 0
    own[...] = jnp.where(first, v[:, 0], v[:, 1]).astype(BF16)[:, None]
    other[...] = jnp.where(first, v[:, 1], v[:, 0]).astype(BF16)[:, None]


def forward_kernel(second_ref, near, far, wg, wu, wd, hh_ref, a_ref, s_ref, out_ref):
    second = second_ref[...] > 0
    x = jnp.where(pl.program_id(0) < 2, near[...], far[...])
    xx = jnp.concatenate(split(x, second), axis=1)
    gate = dot(xx, wg[...], 1, 0)
    up = dot(xx, wu[...], 1, 0)
    sigma = 1.0 / (1.0 + jnp.exp(-gate))
    silu = gate * sigma
    a_ref[...] = up * sigma * (1.0 + gate * (1.0 - sigma))
    s_ref[...] = silu
    hidden = (silu * up).astype(BF16)
    hh = jnp.concatenate(split(hidden, second), axis=1)
    hh_ref[...] = hh
    out_ref[...] = dot(hh, wd[...], 1, 0).astype(BF16).reshape(out_ref.shape)


def down_kernel(core_ref, scale_ref, cots, hh, dout, own, other):
    i = pl.program_id(0)
    ny, nz, rows, _ = cots.shape

    @pl.when(i == 0)
    def _():
        for y in range(ny):
            for z in range(nz):
                at = slice((z * ny + y) * rows, (z * ny + y + 1) * rows)
                dout[at] = (scale_ref[at] * cots[y, z].astype(F32)).astype(BF16)

    columns = pl.ds(pl.multiple_of(i * TILE, TILE), TILE)
    put_grad(dot(dout[:, columns], hh[...], 0, 0), core_ref[0], own, other)


def back_kernel(second_ref, dout, wd, a_ref, s_ref, gu_ref):
    second = second_ref[...] > 0
    ff = a_ref.shape[1]
    both = dot(dout[...], wd[...], 1, 1)
    back = jnp.where(second, both[:, ff:], both[:, :ff])
    gate_grad = (back * a_ref[...]).astype(BF16)
    up_grad = (back * s_ref[...]).astype(BF16)
    gu_ref[...] = jnp.concatenate(split(gate_grad, second) + split(up_grad, second), axis=1)


def weight_kernel(core_ref, near, far, gu, own, other):
    rows = near.shape[0]
    value = dot(near[...], gu[:rows], 0, 0) + dot(far[...], gu[rows:], 0, 0)
    put_grad(value, core_ref[0], own, other)


def input_kernel(gu, wg, wu, near, far):
    ff = wg.shape[2]
    i = pl.program_id(0)
    value = None
    for j, w in enumerate((wg, wu)):
        for e in range(EXP):
            c = (j * EXP + e) * ff
            term = dot(gu[:, c : c + ff], w[e], 1, 1)
            value = term if value is None else value + term
    value = value.astype(BF16).reshape(2, -1, value.shape[1])

    @pl.when(i < 2)
    def _():
        near[pl.ds(2 * i, 2)] = value

    @pl.when(i >= 2)
    def _():
        far[pl.ds(2 * i - 4, 2)] = value


def call(kernel, grid, ins, outs, flops, scalars=0):
    moved = sum(a.size * a.dtype.itemsize for *_, a in ins + outs)
    return pl.pallas_call(
        kernel,
        out_shape=[jax.ShapeDtypeStruct(a.shape, a.dtype) for *_, a in outs],
        grid_spec=pltpu.PrefetchScalarGridSpec(
            num_scalar_prefetch=scalars,
            grid=(grid,),
            in_specs=[pl.BlockSpec(b, m) for b, m, _ in ins],
            out_specs=[pl.BlockSpec(b, m) for b, m, _ in outs],
        ),
        compiler_params=pltpu.CompilerParams(vmem_limit_bytes=26 << 20),
        cost_estimate=pl.CostEstimate(flops=flops, bytes_accessed=moved, transcendentals=0),
    )


def whole(a):
    return (a.shape, lambda i, *_: (0,) * len(a.shape), a)


def tiled(a, axis, size):
    block = tuple(size if d == axis else n for d, n in enumerate(a.shape))
    return (block, lambda i, *_: tuple(i if d == axis else 0 for d in range(len(a.shape))), a)


def sds(shape, dtype):
    return jax.ShapeDtypeStruct(shape, dtype)


def per_device(tokens, cotangent, assign, prob, w_gate, w_up, w_down):
    block, width = tokens.shape
    rows = assign.shape[0]
    ff = w_gate.shape[2]
    own_rows = width // 32
    wide = EXP * ff
    unit = 2 * rows * width * ff * EXP
    second = near_first(assign)
    scale = near_first(prob)
    core = lax.axis_index("core").astype(jnp.int32).reshape(1)
    wg2, wu2 = (w.reshape(EXP * width, ff) for w in (w_gate, w_up))
    wd2 = w_down.reshape(wide, width)
    half = rows // 2

    def pieces_of(columns):
        return [tiled(sds((4, 4, own_rows, columns), BF16), 1, 1)] * 2

    def run(kernel, ins, outs, flops, *scalars):
        return call(kernel, 4, ins, outs, flops, len(scalars))(*scalars, *(a for *_, a in ins))

    far_tokens = send(tokens, "zhi", 1)
    x0 = gather_y(tokens)
    far_tokens, cotangent = tie(far_tokens, cotangent)
    x1 = gather_y(far_tokens)
    far_cot = send(cotangent, "zhi", 1)
    both_cot = jnp.stack([cotangent, far_cot])
    cots = exchange(jnp.broadcast_to(both_cot[None], (SIZES["y"], *both_cot.shape)), "y")

    tile = (TILE, width)
    ins = [tiled(second, 0, TILE)]
    ins += [(tile, lambda i: (jnp.minimum(i, 1), 0), x0), (tile, lambda i: (jnp.maximum(i - 2, 0), 0), x1)]
    ins += [whole(a) for a in (wg2, wu2, wd2)]
    outs = [tiled(sds((rows, wide), BF16), 0, TILE)]
    outs += [tiled(sds((rows, ff), F32), 0, TILE)] * 2
    outs += [((2, 1, block, width), lambda i: (i % 2, i // 2, 0, 0), sds((4, 2, block, width), BF16))]
    hh, act, silu, out = run(forward_kernel, ins, outs, 3 * unit)
    out = exchange(out, "y")

    ins = [whole(a) for a in (scale, cots, hh)]
    outs = [whole(sds((rows, width), BF16)), *pieces_of(wide)]
    dout, down, other = run(down_kernel, ins, outs, unit, core)
    down_c = send(other, "core", 1)

    ins = [tiled(second, 0, TILE), tiled(dout, 0, TILE), whole(wd2), tiled(act, 0, TILE), tiled(silu, 0, TILE)]
    (gu,) = run(back_kernel, ins, [tiled(sds((rows, 2 * wide), BF16), 0, TILE)], unit)

    gu, down_c = tie(gu, down_c)
    down, down_x = pick(add(down.astype(F32), [down_c]), "x")
    gu, down, down_x = tie(gu, down, down_x)
    down_x = sends(down_x, "x")
    ins = [tiled(x0, 1, TILE), tiled(x1, 1, TILE), whole(gu)]
    both, other = run(weight_kernel, ins, pieces_of(2 * wide), 2 * unit, core)
    both_c = send(other, "core", 1)
    out, both = tie(out, both)
    out = total(out)
    out, gu, both = tie(out, gu, both)
    far_out = send(out[1].astype(BF16), "zhi", 1)

    ins = [tiled(gu, 0, TILE), whole(w_gate), whole(w_up)]
    outs = [whole(sds((4, block, width), BF16))] * 2
    near, far = run(input_kernel, ins, outs, 2 * unit)

    near, far, both_c, down_x, far_out = tie(near, far, both_c, down_x, far_out)
    both, both_x = pick(add(both.astype(F32), [both_c]), "x")
    far, near, both, both_x = tie(far, near, both, both_x)
    both_x = sends(both_x, "x")
    far = exchange(far, "y")
    near, far = tie(near, far)
    near = exchange(near, "y")
    far = send(total(far).astype(BF16), "zhi", 1)
    own_scale = lax.dynamic_slice_in_dim(scale, lax.axis_index("y") * block, block)
    output = (add(out[0], [far_out]) * own_scale).astype(BF16)
    down = add(down, down_x)
    grads = jnp.concatenate([down, add(both, both_x)], axis=2).astype(BF16)
    grads, near, far = tie(grads, near, far)
    grads = exchange(grads, "zlo")
    input_grad = add(total(near), [far]).astype(BF16)
    grads = total(grads).reshape(own_rows, 3, EXP, ff)
    return (
        output,
        input_grad,
        grads[:, 1].swapaxes(0, 1),
        grads[:, 2].swapaxes(0, 1),
        grads[:, 0].transpose(1, 2, 0),
    )


def solution(mesh):
    fine = Mesh(mesh.devices.reshape(*SIZES.values()), AXES)
    dp, shard = ("zlo", "x", "core"), ("zhi", "y")
    return jax.shard_map(
        per_device,
        mesh=fine,
        in_specs=(
            P(AXES, None),
            P(AXES, None),
            P(dp),
            P(dp),
            P(None, None, shard),
            P(None, None, shard),
            P(None, shard, None),
        ),
        out_specs=(
            P(AXES, None),
            P(AXES, None),
            P(None, dp, shard),
            P(None, dp, shard),
            P(None, shard, dp),
        ),
        check_vma=False,
    )
```

```python
import jax
import jax.numpy as jnp
from jax import lax
from jax.experimental import pallas as pl
from jax.experimental.pallas import tpu as pltpu
from jax.sharding import Mesh, PartitionSpec as P

EXP = 2
AXES = ("zlo", "x", "core", "zhi", "y")
SIZES = {"zlo": 4, "x": 4, "core": 2, "zhi": 2, "y": 4}
F32, BF16 = jnp.float32, jnp.bfloat16
TILE = 256


def send(value, axis, step):
    n = SIZES[axis]
    return lax.ppermute(value, axis, [(i, (i + step) % n) for i in range(n)])


def tie(*values):
    return lax.optimization_barrier(values)


def exchange(value, axis):
    return lax.all_to_all(value, axis, 0, 0, tiled=True)


def near_first(values):
    v = values.reshape(2, -1)
    return jnp.where(lax.axis_index("zhi") == 0, v, v[::-1]).reshape(-1, 1)


def gather_y(block):
    copies = jnp.broadcast_to(block[None], (SIZES["y"], *block.shape))
    return exchange(copies, "y").reshape(-1, block.shape[-1])


def total(pieces):
    value = pieces[0].astype(F32)
    for k in range(1, pieces.shape[0]):
        value = value + pieces[k].astype(F32)
    return value


def pick(value, axis):
    n = SIZES[axis]
    me = lax.axis_index(axis)
    own = lax.dynamic_index_in_dim(value, me, 0, keepdims=False)
    return own, [lax.dynamic_index_in_dim(value, (me + k) % n, 0, keepdims=False).astype(BF16) for k in range(1, n)]


def sends(pieces, axis):
    return [send(piece, axis, k) for k, piece in enumerate(pieces, 1)]


def add(own, pieces):
    for piece in pieces:
        own = own + piece.astype(F32)
    return own


def dot(a, b, ca, cb):
    return lax.dot_general(a, b, (((ca,), (cb,)), ((), ())), preferred_element_type=F32)


def split(value, second):
    zero = jnp.zeros_like(value)
    return jnp.where(second, zero, value), jnp.where(second, value, zero)


def put_grad(value, core, own, other):
    v = value.reshape(4, 2, value.shape[0] // 8, value.shape[1])
    first = core == 0
    own[...] = jnp.where(first, v[:, 0], v[:, 1]).astype(BF16)[:, None]
    other[...] = jnp.where(first, v[:, 1], v[:, 0]).astype(BF16)[:, None]


def forward_kernel(second_ref, near, far, wg, wu, wd, hh_ref, a_ref, s_ref, out_ref):
    second = second_ref[...] > 0
    x = jnp.where(pl.program_id(0) < 2, near[...], far[...])
    xx = jnp.concatenate(split(x, second), axis=1)
    gate = dot(xx, wg[...], 1, 0)
    up = dot(xx, wu[...], 1, 0)
    sigma = 1.0 / (1.0 + jnp.exp(-gate))
    silu = gate * sigma
    a_ref[...] = (up * sigma * (1.0 + gate * (1.0 - sigma))).astype(BF16)
    s_ref[...] = silu.astype(BF16)
    hidden = (silu * up).astype(BF16)
    hh = jnp.concatenate(split(hidden, second), axis=1)
    hh_ref[...] = hh
    out_ref[...] = dot(hh, wd[...], 1, 0).astype(BF16).reshape(out_ref.shape)


def down_kernel(place, scale_ref, *refs):
    hh, dout, own, other = refs[8:]
    i = pl.program_id(0)
    rows = refs[0].shape[0]

    @pl.when(i == 0)
    def _():
        for j, block in enumerate(refs[:8]):
            y = (place[1] + 4 - j % 4) % 4
            at = pl.ds(pl.multiple_of((j // 4 * 4 + y) * rows, rows), rows)
            dout[at] = (scale_ref[at] * block[...].astype(F32)).astype(BF16)

    columns = pl.ds(pl.multiple_of(i * TILE, TILE), TILE)
    put_grad(dot(dout[:, columns], hh[...], 0, 0), place[0], own, other)


def back_kernel(second_ref, dout, wd, a_ref, s_ref, gu_ref):
    second = second_ref[...] > 0
    ff = a_ref.shape[1]
    both = dot(dout[...], wd[...], 1, 1)
    back = jnp.where(second, both[:, ff:], both[:, :ff])
    gate_grad = (back * a_ref[...]).astype(BF16)
    up_grad = (back * s_ref[...]).astype(BF16)
    gu_ref[...] = jnp.concatenate(split(gate_grad, second) + split(up_grad, second), axis=1)


def weight_kernel(place, near, far, gu, own, other):
    rows = near.shape[0]
    value = dot(near[...], gu[:rows], 0, 0) + dot(far[...], gu[rows:], 0, 0)
    put_grad(value, place[0], own, other)


def input_kernel(gu, wg, wu, out_ref):
    ff = wg.shape[2]
    value = None
    for j, w in enumerate((wg, wu)):
        for e in range(EXP):
            c = (j * EXP + e) * ff
            term = dot(gu[:, c : c + ff], w[e], 1, 1)
            value = term if value is None else value + term
    out_ref[...] = value.astype(BF16).reshape(out_ref.shape)


def call(kernel, grid, ins, outs, flops, scalars=0):
    moved = sum(a.size * a.dtype.itemsize for *_, a in ins + outs)
    return pl.pallas_call(
        kernel,
        out_shape=[jax.ShapeDtypeStruct(a.shape, a.dtype) for *_, a in outs],
        grid_spec=pltpu.PrefetchScalarGridSpec(
            num_scalar_prefetch=scalars,
            grid=(grid,),
            in_specs=[pl.BlockSpec(b, m) for b, m, _ in ins],
            out_specs=[pl.BlockSpec(b, m) for b, m, _ in outs],
        ),
        compiler_params=pltpu.CompilerParams(vmem_limit_bytes=56 << 20),
        cost_estimate=pl.CostEstimate(flops=flops, bytes_accessed=moved, transcendentals=0),
    )


def whole(a):
    return (a.shape, lambda i, *_: (0,) * len(a.shape), a)


def tiled(a, axis, size):
    block = tuple(size if d == axis else n for d, n in enumerate(a.shape))
    return (block, lambda i, *_: tuple(i if d == axis else 0 for d in range(len(a.shape))), a)


def sds(shape, dtype):
    return jax.ShapeDtypeStruct(shape, dtype)


def per_device(tokens, cotangent, assign, prob, w_gate, w_up, w_down):
    block, width = tokens.shape
    rows = assign.shape[0]
    ff = w_gate.shape[2]
    own_rows = width // 32
    wide = EXP * ff
    unit = 2 * rows * width * ff * EXP
    second = near_first(assign)
    scale = near_first(prob)
    place = jnp.stack([lax.axis_index("core"), lax.axis_index("y")]).astype(jnp.int32)
    wg2, wu2 = (w.reshape(EXP * width, ff) for w in (w_gate, w_up))
    wd2 = w_down.reshape(wide, width)

    def pieces_of(columns):
        return [tiled(sds((4, 4, own_rows, columns), BF16), 1, 1)] * 2

    def run(kernel, ins, outs, flops, *scalars, grid=4):
        return call(kernel, grid, ins, outs, flops, len(scalars))(*scalars, *(a for *_, a in ins))

    def inputs(gu, h):
        ins = [((TILE, 2 * wide), lambda i: (i + 2 * h, 0), gu), whole(w_gate), whole(w_up)]
        (part,) = run(input_kernel, ins, [tiled(sds((4, block, width), BF16), 0, 2)], unit, grid=2)
        return part

    far_tokens = send(tokens, "zhi", 1)
    far_cot = send(cotangent, "zhi", 1)
    x0 = gather_y(tokens)
    d0 = sends([cotangent] * 3, "y")
    x0, far_tokens, far_cot, d0 = tie(x0, far_tokens, far_cot, d0)
    x1 = gather_y(far_tokens)
    d1 = sends([far_cot] * 3, "y")

    tile = (TILE, width)
    ins = [tiled(second, 0, TILE)]
    ins += [(tile, lambda i: (jnp.minimum(i, 1), 0), x0), (tile, lambda i: (jnp.maximum(i - 2, 0), 0), x1)]
    ins += [whole(a) for a in (wg2, wu2, wd2)]
    outs = [tiled(sds((rows, wide), BF16), 0, TILE)]
    outs += [tiled(sds((rows, ff), BF16), 0, TILE)] * 2
    outs += [((2, 1, block, width), lambda i: (i % 2, i // 2, 0, 0), sds((4, 2, block, width), BF16))]
    hh, act, silu, out = run(forward_kernel, ins, outs, 3 * unit)
    out = exchange(out, "y")

    ins = [whole(a) for a in (scale, cotangent, *d0, far_cot, *d1, hh)]
    outs = [whole(sds((rows, width), BF16)), *pieces_of(wide)]
    dout, down, other = run(down_kernel, ins, outs, unit, place)
    down_c = send(other, "core", 1)

    ins = [tiled(second, 0, TILE), tiled(dout, 0, TILE), whole(wd2), tiled(act, 0, TILE), tiled(silu, 0, TILE)]
    (gu,) = run(back_kernel, ins, [tiled(sds((rows, 2 * wide), BF16), 0, TILE)], unit)
    far = inputs(gu, 1)

    far, out, down_c = tie(far, out, down_c)
    down, down_x = pick(add(down.astype(F32), [down_c]), "x")
    out = total(out)
    far, out, down, down_x, gu = tie(far, out, down, down_x, gu)
    far = exchange(far, "y")
    down_x = sends(down_x, "x")
    far_out = send(out[1].astype(BF16), "zhi", 1)

    ins = [tiled(x0, 1, TILE), tiled(x1, 1, TILE), whole(gu)]
    both, other = run(weight_kernel, ins, pieces_of(2 * wide), 2 * unit, place)
    both_c = send(other, "core", 1)
    both, gu = tie(both, gu)
    near = inputs(gu, 0)

    near, far, both_c, down_x, far_out = tie(near, far, both_c, down_x, far_out)
    both, both_x = pick(add(both.astype(F32), [both_c]), "x")
    far = total(far).astype(BF16)
    near, far, both, both_x = tie(near, far, both, both_x)
    both_x = sends(both_x, "x")
    far = send(far, "zhi", 1)
    near = exchange(near, "y")
    own_scale = lax.dynamic_slice_in_dim(scale, lax.axis_index("y") * block, block)
    output = (add(out[0], [far_out]) * own_scale).astype(BF16)
    down = add(down, down_x)
    down, near, far, both_x = tie(down, near, far, both_x)
    grads = jnp.concatenate([down, add(both, both_x)], axis=2).astype(BF16)
    grads = exchange(grads, "zlo")
    input_grad = add(total(near), [far]).astype(BF16)
    grads = total(grads).reshape(own_rows, 3, EXP, ff)
    return (
        output,
        input_grad,
        grads[:, 1].swapaxes(0, 1),
        grads[:, 2].swapaxes(0, 1),
        grads[:, 0].transpose(1, 2, 0),
    )


def solution(mesh):
    fine = Mesh(mesh.devices.reshape(*SIZES.values()), AXES)
    dp, shard = ("zlo", "x", "core"), ("zhi", "y")
    return jax.shard_map(
        per_device,
        mesh=fine,
        in_specs=(
            P(AXES, None),
            P(AXES, None),
            P(dp),
            P(dp),
            P(None, None, shard),
            P(None, None, shard),
            P(None, shard, None),
        ),
        out_specs=(
            P(AXES, None),
            P(AXES, None),
            P(None, dp, shard),
            P(None, dp, shard),
            P(None, shard, dp),
        ),
        check_vma=False,
    )
```

```python
import jax
import jax.numpy as jnp
from jax import lax
from jax.experimental import pallas as pl
from jax.experimental.pallas import tpu as pltpu
from jax.sharding import Mesh, PartitionSpec as P

EXP = 2
AXES = ("zlo", "x", "core", "zhi", "y")
SIZES = {"zlo": 4, "x": 4, "core": 2, "zhi": 2, "y": 4}
F32, BF16 = jnp.float32, jnp.bfloat16
TILE = 256


def send(value, axis, step):
    n = SIZES[axis]
    return lax.ppermute(value, axis, [(i, (i + step) % n) for i in range(n)])


def relative(values):
    rows = values.shape[0] // 8
    blocks = values.reshape(2, 4, rows)[:, ::-1]
    doubled = jnp.tile(blocks, (2, 2, 1))
    start = (lax.axis_index("zhi"), 3 - lax.axis_index("y"), 0)
    return lax.dynamic_slice(doubled, start, (2, 4, rows)).reshape(-1, 1)


def gather_group(block):
    far = send(block, "zhi", 1)
    parts = []
    for b in (block, far):
        parts += [b, send(b, "y", 1), send(b, "y", 2), send(b, "y", 3)]
    return parts


def tie(*values):
    return lax.optimization_barrier(values)


def sends(pieces, axis, way=1):
    return [send(piece, axis, way * k) for k, piece in enumerate(pieces, 1)]


def add(own, pieces):
    for piece in pieces:
        own = own + piece.astype(F32)
    return own


def pick(value, axis):
    n = SIZES[axis]
    me = lax.axis_index(axis)
    own = lax.dynamic_index_in_dim(value, me, 0, keepdims=False)
    return own, [lax.dynamic_index_in_dim(value, (me + k) % n, 0, keepdims=False).astype(BF16) for k in range(1, n)]


def dot(a, b, ca, cb):
    return lax.dot_general(a, b, (((ca,), (cb,)), ((), ())), preferred_element_type=F32)


def split(value, second):
    zero = jnp.zeros_like(value)
    return jnp.where(second, zero, value), jnp.where(second, value, zero)


def put_rows(value, own, s1, s2, s3):
    i = pl.program_id(0)
    half = value.shape[0] // 2

    @pl.when(i % 2 == 0)
    def _():
        own[pl.ds(i // 2, 1)] = value[:half][None]
        s1[pl.ds(i // 2, 1)] = value[half:].astype(BF16)[None]

    @pl.when(i % 2 == 1)
    def _():
        s2[pl.ds(i // 2, 1)] = value[:half].astype(BF16)[None]
        s3[pl.ds(i // 2, 1)] = value[half:].astype(BF16)[None]


def put_grad(value, core, own, other):
    v = value.reshape(4, 2, value.shape[0] // 8, value.shape[1])
    first = core == 0
    own[...] = jnp.where(first, v[:, 0], v[:, 1]).astype(BF16)[:, None]
    other[...] = jnp.where(first, v[:, 1], v[:, 0]).astype(BF16)[:, None]


def forward_kernel(second_ref, *refs):
    blocks = refs[:8]
    wg, wu, wd, x_ref, hh_ref, a_ref, s_ref = refs[8:15]
    i = pl.program_id(0)
    n = blocks[0].shape[0]

    @pl.when(i == 0)
    def _():
        for b, block in enumerate(blocks):
            x_ref[b * n : (b + 1) * n] = block[...]

    rows = pl.ds(pl.multiple_of(i * TILE, TILE), TILE)
    second = second_ref[rows] > 0
    x0, x1 = split(x_ref[rows], second)
    xx = jnp.concatenate([x0, x1], axis=1)
    gate = dot(xx, wg[...], 1, 0)
    up = dot(xx, wu[...], 1, 0)
    sigma = 1.0 / (1.0 + jnp.exp(-gate))
    silu = gate * sigma
    a_ref[...] = up * sigma * (1.0 + gate * (1.0 - sigma))
    s_ref[...] = silu
    hidden = (silu * up).astype(BF16)
    hh = jnp.concatenate(split(hidden, second), axis=1)
    hh_ref[...] = hh
    put_rows(dot(hh, wd[...], 1, 0), *refs[15:19])


def back_kernel(second_ref, scale_ref, *refs):
    a_ref, s_ref, wd, dout, gu_ref = refs[4:]
    i = pl.program_id(0)
    n = refs[0].shape[1]

    @pl.when(i == 0)
    def _():
        for b in range(8):
            at = slice(b * n, (b + 1) * n)
            dout[at] = (scale_ref[at] * refs[b % 4][b // 4].astype(F32)).astype(BF16)

    rows = pl.ds(pl.multiple_of(i * TILE, TILE), TILE)
    second = second_ref[...] > 0
    ff = a_ref.shape[1]
    both = dot(dout[rows], wd[...], 1, 1)
    back = jnp.where(second, both[:, ff:], both[:, :ff])
    gate_grad = (back * a_ref[...]).astype(BF16)
    up_grad = (back * s_ref[...]).astype(BF16)
    gu_ref[...] = jnp.concatenate(split(gate_grad, second) + split(up_grad, second), axis=1)


def outer_kernel(core_ref, left, right, own, other):
    put_grad(dot(left[...], right[...], 0, 0), core_ref[0], own, other)


def input_kernel(gu, wg, wu, *outs):
    ff = wg.shape[2]
    total = None
    for j, w in enumerate((wg, wu)):
        for e in range(EXP):
            c = (j * EXP + e) * ff
            term = dot(gu[:, c : c + ff], w[e], 1, 1)
            total = term if total is None else total + term
    put_rows(total, *outs)


def call(kernel, grid, ins, outs, flops, scalars=0):
    return pl.pallas_call(
        kernel,
        out_shape=[jax.ShapeDtypeStruct(a.shape, a.dtype) for *_, a in outs],
        grid_spec=pltpu.PrefetchScalarGridSpec(
            num_scalar_prefetch=scalars,
            grid=(grid,),
            in_specs=[pl.BlockSpec(b, m) for b, m, _ in ins],
            out_specs=[pl.BlockSpec(b, m) for b, m, _ in outs],
        ),
        compiler_params=pltpu.CompilerParams(vmem_limit_bytes=56 << 20),
        cost_estimate=pl.CostEstimate(flops=flops, bytes_accessed=flops // 400, transcendentals=0),
    )


def whole(a):
    return (a.shape, lambda i, *_: (0,) * len(a.shape), a)


def tiled(a, axis, size):
    block = tuple(size if d == axis else n for d, n in enumerate(a.shape))
    return (block, lambda i, *_: tuple(i if d == axis else 0 for d in range(len(a.shape))), a)


def sds(shape, dtype):
    return jax.ShapeDtypeStruct(shape, dtype)


def per_device(tokens, cotangent, assign, prob, w_gate, w_up, w_down):
    block, width = tokens.shape
    rows = assign.shape[0]
    ff = w_gate.shape[2]
    steps = rows // TILE
    own_rows = width // 32
    wide = EXP * ff
    unit = 2 * rows * width * ff * EXP
    second = relative(assign)
    scale = relative(prob)
    core = lax.axis_index("core").astype(jnp.int32).reshape(1)
    xs = gather_group(tokens)
    pair = jnp.stack([cotangent, send(cotangent, "zhi", 1)])
    ds = [pair, *sends([pair] * 3, "y")]
    wg2, wu2 = (w.reshape(EXP * width, ff) for w in (w_gate, w_up))
    wd2 = w_down.reshape(wide, width)
    pieces = [whole(sds((2, block, width), t)) for t in (F32, BF16, BF16, BF16)]

    def run(kernel, ins, outs, flops, *scalars):
        return call(kernel, 4, ins, outs, flops, len(scalars))(*scalars, *(a for *_, a in ins))

    def outer(left, right, cost):
        columns = right.shape[1]
        outs = [tiled(sds((4, 4, own_rows, columns), BF16), 1, 1)] * 2
        own, other = run(outer_kernel, [tiled(left, 1, TILE), whole(right)], outs, cost, core)
        return own, send(other, "core", 1)

    ins = [whole(a) for a in (second, *xs, wg2, wu2, wd2)]
    outs = [
        whole(sds((rows, width), BF16)),
        tiled(sds((rows, wide), BF16), 0, TILE),
        tiled(sds((rows, ff), F32), 0, TILE),
        tiled(sds((rows, ff), F32), 0, TILE),
        *pieces,
    ]
    x, hh, act, silu, out, *out_y = run(forward_kernel, ins, outs, 3 * unit)
    ds, out_y = tie(ds, out_y)
    out_y = sends(out_y, "y", -1)

    ins = [tiled(second, 0, TILE), whole(scale), *(whole(a) for a in ds)]
    ins += [tiled(act, 0, TILE), tiled(silu, 0, TILE), whole(wd2)]
    outs = [whole(sds((rows, width), BF16)), tiled(sds((rows, 2 * wide), BF16), 0, TILE)]
    dout, gu = run(back_kernel, ins, outs, unit // 20)
    both, both_c = outer(x, gu, unit // 10)
    out, out_y, both, dout = tie(out, out_y, both, dout)
    out = add(out, out_y)
    out, dout, both = tie(out, dout, both)
    far_out = send(out[1].astype(BF16), "zhi", 1)
    down, down_c = outer(dout, hh, 8 * unit)
    down, both_c, gu, both = tie(down, both_c, gu, both)
    both, both_x = pick(add(both.astype(F32), [both_c]), "x")
    gu, both, both_x = tie(gu, both, both_x)
    both_x = sends(both_x, "x")

    ins = [tiled(gu, 0, TILE), whole(w_gate), whole(w_up)]
    near, *in_y = run(input_kernel, ins, pieces, 8 * unit)
    near, in_y, down_c, far_out, both_x[0], both_x[2] = tie(near, in_y, down_c, far_out, both_x[0], both_x[2])
    in_y = sends(in_y, "y", -1)
    down, down_x = pick(add(down.astype(F32), [down_c]), "x")
    output = ((out[0] + far_out.astype(F32)) * scale[:block]).astype(BF16)
    down, down_x, both, both_x, output = tie(down, down_x, both, both_x, output)
    down_x = sends(down_x, "x")
    both, both_z = pick(add(both, both_x), "zlo")
    both, both_z, near, in_y = tie(both, both_z, near, in_y)
    both_z = sends(both_z, "zlo")
    near = add(near, in_y)
    down_x[0], near, down = tie(down_x[0], near, down)
    far = send(near[1].astype(BF16), "zhi", 1)
    down, down_z = pick(add(down, down_x), "zlo")
    down, down_z, both, both_z = tie(down, down_z, both, both_z)
    down_z = sends(down_z, "zlo")
    both = add(both, both_z).reshape(own_rows, 2, EXP, ff)
    input_grad = near[0] + far.astype(F32)
    grad_down = add(down, down_z).reshape(own_rows, EXP, ff)
    return (
        output.astype(BF16),
        input_grad.astype(BF16),
        both[:, 0].swapaxes(0, 1),
        both[:, 1].swapaxes(0, 1),
        grad_down.transpose(1, 2, 0),
    )


def solution(mesh):
    fine = Mesh(mesh.devices.reshape(*SIZES.values()), AXES)
    dp, shard = ("zlo", "x", "core"), ("zhi", "y")
    return jax.shard_map(
        per_device,
        mesh=fine,
        in_specs=(
            P(AXES, None),
            P(AXES, None),
            P(dp),
            P(dp),
            P(None, None, shard),
            P(None, None, shard),
            P(None, shard, None),
        ),
        out_specs=(
            P(AXES, None),
            P(AXES, None),
            P(None, dp, shard),
            P(None, dp, shard),
            P(None, shard, dp),
        ),
        check_vma=False,
    )
```

```python
import jax
import jax.numpy as jnp
from jax import lax
from jax.experimental import pallas as pl
from jax.experimental.pallas import tpu as pltpu
from jax.sharding import Mesh, PartitionSpec as P

EXP = 2
AXES = ("zlo", "x", "core", "zhi", "y")
SIZES = {"zlo": 4, "x": 4, "core": 2, "zhi": 2, "y": 4}
F32, BF16 = jnp.float32, jnp.bfloat16
TILE = 256


def send(value, axis, step):
    n = SIZES[axis]
    return lax.ppermute(value, axis, [(i, (i + step) % n) for i in range(n)])


def relative(values):
    rows = values.shape[0] // 8
    blocks = values.reshape(2, 4, rows)[:, ::-1]
    doubled = jnp.tile(blocks, (2, 2, 1))
    start = (lax.axis_index("zhi"), 3 - lax.axis_index("y"), 0)
    return lax.dynamic_slice(doubled, start, (2, 4, rows)).reshape(-1, 1)


def gather_group(block):
    far = send(block, "zhi", 1)
    parts = []
    for b in (block, far):
        parts += [b, send(b, "y", 1), send(b, "y", 2), send(b, "y", 3)]
    return parts


def tie(*values):
    return lax.optimization_barrier(values)


def exchange(value, axis):
    return lax.all_to_all(value, axis, 0, 0, tiled=True)


def sends(pieces, axis, way=1):
    return [send(piece, axis, way * k) for k, piece in enumerate(pieces, 1)]


def add(own, pieces):
    for piece in pieces:
        own = own + piece.astype(F32)
    return own


def pick(value, axis):
    n = SIZES[axis]
    me = lax.axis_index(axis)
    own = lax.dynamic_index_in_dim(value, me, 0, keepdims=False)
    return own, [lax.dynamic_index_in_dim(value, (me + k) % n, 0, keepdims=False).astype(BF16) for k in range(1, n)]


def dot(a, b, ca, cb):
    return lax.dot_general(a, b, (((ca,), (cb,)), ((), ())), preferred_element_type=F32)


def split(value, second):
    zero = jnp.zeros_like(value)
    return jnp.where(second, zero, value), jnp.where(second, value, zero)


def put_rows(value, own, s1, s2, s3):
    i = pl.program_id(0)
    half = value.shape[0] // 2

    @pl.when(i % 2 == 0)
    def _():
        own[pl.ds(i // 2, 1)] = value[:half][None]
        s1[pl.ds(i // 2, 1)] = value[half:].astype(BF16)[None]

    @pl.when(i % 2 == 1)
    def _():
        s2[pl.ds(i // 2, 1)] = value[:half].astype(BF16)[None]
        s3[pl.ds(i // 2, 1)] = value[half:].astype(BF16)[None]


def put_grad(value, core, own, other):
    v = value.reshape(4, 2, value.shape[0] // 8, value.shape[1])
    first = core == 0
    own[...] = jnp.where(first, v[:, 0], v[:, 1]).astype(BF16)[:, None]
    other[...] = jnp.where(first, v[:, 1], v[:, 0]).astype(BF16)[:, None]


def forward_kernel(second_ref, *refs):
    blocks = refs[:8]
    wg, wu, wd, x_ref, hh_ref, a_ref, s_ref = refs[8:15]
    i = pl.program_id(0)
    n = blocks[0].shape[0]

    @pl.when(i == 0)
    def _():
        for b, block in enumerate(blocks):
            x_ref[b * n : (b + 1) * n] = block[...]

    rows = pl.ds(pl.multiple_of(i * TILE, TILE), TILE)
    second = second_ref[rows] > 0
    x0, x1 = split(x_ref[rows], second)
    xx = jnp.concatenate([x0, x1], axis=1)
    gate = dot(xx, wg[...], 1, 0)
    up = dot(xx, wu[...], 1, 0)
    sigma = 1.0 / (1.0 + jnp.exp(-gate))
    silu = gate * sigma
    a_ref[...] = up * sigma * (1.0 + gate * (1.0 - sigma))
    s_ref[...] = silu
    hidden = (silu * up).astype(BF16)
    hh = jnp.concatenate(split(hidden, second), axis=1)
    hh_ref[...] = hh
    put_rows(dot(hh, wd[...], 1, 0), *refs[15:19])


def back_kernel(second_ref, scale_ref, *refs):
    a_ref, s_ref, wd, dout, gu_ref = refs[4:]
    i = pl.program_id(0)
    n = refs[0].shape[1]

    @pl.when(i == 0)
    def _():
        for b in range(8):
            at = slice(b * n, (b + 1) * n)
            dout[at] = (scale_ref[at] * refs[b % 4][b // 4].astype(F32)).astype(BF16)

    rows = pl.ds(pl.multiple_of(i * TILE, TILE), TILE)
    second = second_ref[...] > 0
    ff = a_ref.shape[1]
    both = dot(dout[rows], wd[...], 1, 1)
    back = jnp.where(second, both[:, ff:], both[:, :ff])
    gate_grad = (back * a_ref[...]).astype(BF16)
    up_grad = (back * s_ref[...]).astype(BF16)
    gu_ref[...] = jnp.concatenate(split(gate_grad, second) + split(up_grad, second), axis=1)


def outer_kernel(core_ref, left, right, own, other):
    put_grad(dot(left[...], right[...], 0, 0), core_ref[0], own, other)


def input_kernel(gu, wg, wu, *outs):
    ff = wg.shape[2]
    total = None
    for j, w in enumerate((wg, wu)):
        for e in range(EXP):
            c = (j * EXP + e) * ff
            term = dot(gu[:, c : c + ff], w[e], 1, 1)
            total = term if total is None else total + term
    put_rows(total, *outs)


def call(kernel, grid, ins, outs, flops, scalars=0):
    return pl.pallas_call(
        kernel,
        out_shape=[jax.ShapeDtypeStruct(a.shape, a.dtype) for *_, a in outs],
        grid_spec=pltpu.PrefetchScalarGridSpec(
            num_scalar_prefetch=scalars,
            grid=(grid,),
            in_specs=[pl.BlockSpec(b, m) for b, m, _ in ins],
            out_specs=[pl.BlockSpec(b, m) for b, m, _ in outs],
        ),
        compiler_params=pltpu.CompilerParams(vmem_limit_bytes=56 << 20),
        cost_estimate=pl.CostEstimate(flops=flops, bytes_accessed=flops // 400, transcendentals=0),
    )


def whole(a):
    return (a.shape, lambda i, *_: (0,) * len(a.shape), a)


def tiled(a, axis, size):
    block = tuple(size if d == axis else n for d, n in enumerate(a.shape))
    return (block, lambda i, *_: tuple(i if d == axis else 0 for d in range(len(a.shape))), a)


def sds(shape, dtype):
    return jax.ShapeDtypeStruct(shape, dtype)


def per_device(tokens, cotangent, assign, prob, w_gate, w_up, w_down):
    block, width = tokens.shape
    rows = assign.shape[0]
    ff = w_gate.shape[2]
    steps = rows // TILE
    own_rows = width // 32
    wide = EXP * ff
    unit = 2 * rows * width * ff * EXP
    second = relative(assign)
    scale = relative(prob)
    core = lax.axis_index("core").astype(jnp.int32).reshape(1)
    xs = gather_group(tokens)
    pair = jnp.stack([cotangent, send(cotangent, "zhi", 1)])
    ds = [pair, *sends([pair] * 3, "y")]
    wg2, wu2 = (w.reshape(EXP * width, ff) for w in (w_gate, w_up))
    wd2 = w_down.reshape(wide, width)
    pieces = [whole(sds((2, block, width), t)) for t in (F32, BF16, BF16, BF16)]

    def run(kernel, ins, outs, flops, *scalars):
        return call(kernel, 4, ins, outs, flops, len(scalars))(*scalars, *(a for *_, a in ins))

    def outer(left, right, cost):
        columns = right.shape[1]
        outs = [tiled(sds((4, 4, own_rows, columns), BF16), 1, 1)] * 2
        own, other = run(outer_kernel, [tiled(left, 1, TILE), whole(right)], outs, cost, core)
        return own, send(other, "core", 1)

    ins = [whole(a) for a in (second, *xs, wg2, wu2, wd2)]
    outs = [
        whole(sds((rows, width), BF16)),
        tiled(sds((rows, wide), BF16), 0, TILE),
        tiled(sds((rows, ff), F32), 0, TILE),
        tiled(sds((rows, ff), F32), 0, TILE),
        *pieces,
    ]
    x, hh, act, silu, out, *out_y = run(forward_kernel, ins, outs, 3 * unit)
    ds, out_y = tie(ds, out_y)
    out_y = sends(out_y, "y", -1)

    ins = [tiled(second, 0, TILE), whole(scale), *(whole(a) for a in ds)]
    ins += [tiled(act, 0, TILE), tiled(silu, 0, TILE), whole(wd2)]
    outs = [whole(sds((rows, width), BF16)), tiled(sds((rows, 2 * wide), BF16), 0, TILE)]
    dout, gu = run(back_kernel, ins, outs, unit // 20)
    both, both_c = outer(x, gu, unit // 10)
    out, out_y, both, dout = tie(out, out_y, both, dout)
    out = add(out, out_y)
    out, dout, both = tie(out, dout, both)
    far_out = send(out[1].astype(BF16), "zhi", 1)
    down, down_c = outer(dout, hh, 8 * unit)
    down, both_c, gu, both = tie(down, both_c, gu, both)
    both, both_x = pick(add(both.astype(F32), [both_c]), "x")
    gu, both, both_x = tie(gu, both, both_x)
    both_x = sends(both_x, "x")

    ins = [tiled(gu, 0, TILE), whole(w_gate), whole(w_up)]
    near, *in_y = run(input_kernel, ins, pieces, 8 * unit)
    near, in_y, down_c, far_out, both_x[0], both_x[2] = tie(near, in_y, down_c, far_out, both_x[0], both_x[2])
    in_y = sends(in_y, "y", -1)
    down, down_x = pick(add(down.astype(F32), [down_c]), "x")
    output = (out[0] + far_out.astype(F32)) * scale[:block]
    down, down_x, both, both_x, output, in_y[0], in_y[2] = tie(down, down_x, both, both_x, output, in_y[0], in_y[2])
    down_x = sends(down_x, "x")
    both = exchange(add(both, both_x).astype(BF16), "zlo")
    down, down_x, both, near, in_y[1] = tie(down, down_x, both, near, in_y[1])
    near = add(near, in_y)
    far = send(near[1].astype(BF16), "zhi", 1)
    down = exchange(add(down, down_x).astype(BF16), "zlo")
    both = add(both[0].astype(F32), both[1:]).reshape(own_rows, 2, EXP, ff)
    input_grad = near[0] + far.astype(F32)
    grad_down = add(down[0].astype(F32), down[1:]).reshape(own_rows, EXP, ff)
    return (
        output.astype(BF16),
        input_grad.astype(BF16),
        both[:, 0].swapaxes(0, 1),
        both[:, 1].swapaxes(0, 1),
        grad_down.transpose(1, 2, 0),
    )


def solution(mesh):
    fine = Mesh(mesh.devices.reshape(*SIZES.values()), AXES)
    dp, shard = ("zlo", "x", "core"), ("zhi", "y")
    return jax.shard_map(
        per_device,
        mesh=fine,
        in_specs=(
            P(AXES, None),
            P(AXES, None),
            P(dp),
            P(dp),
            P(None, None, shard),
            P(None, None, shard),
            P(None, shard, None),
        ),
        out_specs=(
            P(AXES, None),
            P(AXES, None),
            P(None, dp, shard),
            P(None, dp, shard),
            P(None, shard, dp),
        ),
        check_vma=False,
    )
```

```python
import jax
import jax.numpy as jnp
from jax import lax
from jax.experimental import pallas as pl
from jax.experimental.pallas import tpu as pltpu
from jax.sharding import Mesh, PartitionSpec as P

EXP = 2
AXES = ("zlo", "x", "core", "zhi", "y")
SIZES = {"zlo": 4, "x": 4, "core": 2, "zhi": 2, "y": 4}
F32, BF16 = jnp.float32, jnp.bfloat16
TILE = 256


def send(value, axis, step):
    n = SIZES[axis]
    return lax.ppermute(value, axis, [(i, (i + step) % n) for i in range(n)])


def relative(values):
    rows = values.shape[0] // 8
    blocks = values.reshape(2, 4, rows)[:, ::-1]
    doubled = jnp.tile(blocks, (2, 2, 1))
    start = (lax.axis_index("zhi"), 3 - lax.axis_index("y"), 0)
    return lax.dynamic_slice(doubled, start, (2, 4, rows)).reshape(-1, 1)


def tie(*values):
    return lax.optimization_barrier(values)


def exchange(value, axis):
    return lax.all_to_all(value, axis, 0, 0, tiled=True)


def sends(pieces, axis, way=1):
    return [send(piece, axis, way * k) for k, piece in enumerate(pieces, 1)]


def add(own, pieces):
    for piece in pieces:
        own = own + piece.astype(F32)
    return own


def pick(value, axis):
    n = SIZES[axis]
    me = lax.axis_index(axis)
    own = lax.dynamic_index_in_dim(value, me, 0, keepdims=False)
    return own, [lax.dynamic_index_in_dim(value, (me + k) % n, 0, keepdims=False).astype(BF16) for k in range(1, n)]


def dot(a, b, ca, cb):
    return lax.dot_general(a, b, (((ca,), (cb,)), ((), ())), preferred_element_type=F32)


def split(value, second):
    zero = jnp.zeros_like(value)
    return jnp.where(second, zero, value), jnp.where(second, value, zero)


def put_rows(value, own, s1, s2, s3):
    i = pl.program_id(0)
    half = value.shape[0] // 2

    @pl.when(i % 2 == 0)
    def _():
        own[pl.ds(i // 2, 1)] = value[:half][None]
        s1[pl.ds(i // 2, 1)] = value[half:].astype(BF16)[None]

    @pl.when(i % 2 == 1)
    def _():
        s2[pl.ds(i // 2, 1)] = value[:half].astype(BF16)[None]
        s3[pl.ds(i // 2, 1)] = value[half:].astype(BF16)[None]


def put_grad(value, core, own, other):
    v = value.reshape(4, 2, value.shape[0] // 8, value.shape[1])
    first = core == 0
    own[...] = jnp.where(first, v[:, 0], v[:, 1]).astype(BF16)[:, None]
    other[...] = jnp.where(first, v[:, 1], v[:, 0]).astype(BF16)[:, None]


def forward_kernel(second_ref, *refs):
    blocks = refs[:8]
    wg, wu, wd, x_ref, hh_ref, a_ref, s_ref = refs[8:15]
    i = pl.program_id(0)
    n = blocks[0].shape[0]

    @pl.when(i == 0)
    def _():
        for b, block in enumerate(blocks):
            x_ref[b * n : (b + 1) * n] = block[...]

    rows = pl.ds(pl.multiple_of(i * TILE, TILE), TILE)
    second = second_ref[rows] > 0
    x0, x1 = split(x_ref[rows], second)
    xx = jnp.concatenate([x0, x1], axis=1)
    gate = dot(xx, wg[...], 1, 0)
    up = dot(xx, wu[...], 1, 0)
    sigma = 1.0 / (1.0 + jnp.exp(-gate))
    silu = gate * sigma
    a_ref[...] = up * sigma * (1.0 + gate * (1.0 - sigma))
    s_ref[...] = silu
    hidden = (silu * up).astype(BF16)
    hh = jnp.concatenate(split(hidden, second), axis=1)
    hh_ref[...] = hh
    put_rows(dot(hh, wd[...], 1, 0), *refs[15:19])


def back_kernel(second_ref, scale_ref, *refs):
    a_ref, s_ref, wd, dout, gu_ref = refs[8:]
    i = pl.program_id(0)
    n = refs[0].shape[0]

    @pl.when(i == 0)
    def _():
        for b, block in enumerate(refs[:8]):
            at = slice(b * n, (b + 1) * n)
            dout[at] = (scale_ref[at] * block[...].astype(F32)).astype(BF16)

    rows = pl.ds(pl.multiple_of(i * TILE, TILE), TILE)
    second = second_ref[...] > 0
    ff = a_ref.shape[1]
    both = dot(dout[rows], wd[...], 1, 1)
    back = jnp.where(second, both[:, ff:], both[:, :ff])
    gate_grad = (back * a_ref[...]).astype(BF16)
    up_grad = (back * s_ref[...]).astype(BF16)
    gu_ref[...] = jnp.concatenate(split(gate_grad, second) + split(up_grad, second), axis=1)


def outer_kernel(core_ref, left, right, own, other):
    put_grad(dot(left[...], right[...], 0, 0), core_ref[0], own, other)


def input_kernel(gu, wg, wu, *outs):
    ff = wg.shape[2]
    total = None
    for j, w in enumerate((wg, wu)):
        for e in range(EXP):
            c = (j * EXP + e) * ff
            term = dot(gu[:, c : c + ff], w[e], 1, 1)
            total = term if total is None else total + term
    put_rows(total, *outs)


def call(kernel, grid, ins, outs, flops, scalars=0):
    return pl.pallas_call(
        kernel,
        out_shape=[jax.ShapeDtypeStruct(a.shape, a.dtype) for *_, a in outs],
        grid_spec=pltpu.PrefetchScalarGridSpec(
            num_scalar_prefetch=scalars,
            grid=(grid,),
            in_specs=[pl.BlockSpec(b, m) for b, m, _ in ins],
            out_specs=[pl.BlockSpec(b, m) for b, m, _ in outs],
        ),
        compiler_params=pltpu.CompilerParams(vmem_limit_bytes=56 << 20),
        cost_estimate=pl.CostEstimate(flops=flops, bytes_accessed=flops // 400, transcendentals=0),
    )


def whole(a):
    return (a.shape, lambda i, *_: (0,) * len(a.shape), a)


def tiled(a, axis, size):
    block = tuple(size if d == axis else n for d, n in enumerate(a.shape))
    return (block, lambda i, *_: tuple(i if d == axis else 0 for d in range(len(a.shape))), a)


def sds(shape, dtype):
    return jax.ShapeDtypeStruct(shape, dtype)


def per_device(tokens, cotangent, assign, prob, w_gate, w_up, w_down):
    block, width = tokens.shape
    rows = assign.shape[0]
    ff = w_gate.shape[2]
    steps = rows // TILE
    own_rows = width // 32
    wide = EXP * ff
    unit = 2 * rows * width * ff * EXP
    second = relative(assign)
    scale = relative(prob)
    core = lax.axis_index("core").astype(jnp.int32).reshape(1)
    far_tokens, far_cot = send(tokens, "zhi", 1), send(cotangent, "zhi", 1)
    x0 = sends([tokens] * 3, "y")
    d0 = [send(cotangent, "y", 1)]
    far_tokens, d0[0] = tie(far_tokens, d0[0])
    d0 += [send(cotangent, "y", k) for k in (2, 3)]
    xs = [tokens, *x0, far_tokens, *sends([far_tokens] * 3, "y")]
    ds = [cotangent, *d0, far_cot, *sends([far_cot] * 3, "y")]
    wg2, wu2 = (w.reshape(EXP * width, ff) for w in (w_gate, w_up))
    wd2 = w_down.reshape(wide, width)
    pieces = [whole(sds((2, block, width), t)) for t in (F32, BF16, BF16, BF16)]

    def run(kernel, ins, outs, flops, *scalars):
        return call(kernel, 4, ins, outs, flops, len(scalars))(*scalars, *(a for *_, a in ins))

    def outer(left, right, cost):
        columns = right.shape[1]
        outs = [tiled(sds((4, 4, own_rows, columns), BF16), 1, 1)] * 2
        own, other = run(outer_kernel, [tiled(left, 1, TILE), whole(right)], outs, cost, core)
        return own, send(other, "core", 1)

    ins = [whole(a) for a in (second, *xs, wg2, wu2, wd2)]
    outs = [
        whole(sds((rows, width), BF16)),
        tiled(sds((rows, wide), BF16), 0, TILE),
        tiled(sds((rows, ff), F32), 0, TILE),
        tiled(sds((rows, ff), F32), 0, TILE),
        *pieces,
    ]
    x, hh, act, silu, out, *out_y = run(forward_kernel, ins, outs, 3 * unit)
    ds, out_y = tie(ds, out_y)
    out_y = sends(out_y, "y", -1)

    ins = [tiled(second, 0, TILE), whole(scale), *(whole(a) for a in ds)]
    ins += [tiled(act, 0, TILE), tiled(silu, 0, TILE), whole(wd2)]
    outs = [whole(sds((rows, width), BF16)), tiled(sds((rows, 2 * wide), BF16), 0, TILE)]
    dout, gu = run(back_kernel, ins, outs, unit // 20)
    both, both_c = outer(x, gu, unit // 10)
    out, out_y, both, dout = tie(out, out_y, both, dout)
    out = add(out, out_y)
    out, dout, both = tie(out, dout, both)
    far_out = send(out[1].astype(BF16), "zhi", 1)
    down, down_c = outer(dout, hh, 8 * unit)
    down, both_c, gu, both = tie(down, both_c, gu, both)
    both, both_x = pick(add(both.astype(F32), [both_c]), "x")
    gu, both, both_x = tie(gu, both, both_x)
    both_x = sends(both_x, "x")

    ins = [tiled(gu, 0, TILE), whole(w_gate), whole(w_up)]
    near, *in_y = run(input_kernel, ins, pieces, 8 * unit)
    near, in_y, down_c, far_out, both_x[0], both_x[2] = tie(near, in_y, down_c, far_out, both_x[0], both_x[2])
    in_y = sends(in_y, "y", -1)
    down, down_x = pick(add(down.astype(F32), [down_c]), "x")
    output = (out[0] + far_out.astype(F32)) * scale[:block]
    down, down_x, both, both_x, output, in_y[0], in_y[2] = tie(down, down_x, both, both_x, output, in_y[0], in_y[2])
    down_x = sends(down_x, "x")
    both = exchange(add(both, both_x).astype(BF16), "zlo")
    down, down_x, both, near, in_y[1] = tie(down, down_x, both, near, in_y[1])
    near = add(near, in_y)
    far = send(near[1].astype(BF16), "zhi", 1)
    down = exchange(add(down, down_x).astype(BF16), "zlo")
    both = add(both[0].astype(F32), both[1:]).reshape(own_rows, 2, EXP, ff)
    input_grad = near[0] + far.astype(F32)
    grad_down = add(down[0].astype(F32), down[1:]).reshape(own_rows, EXP, ff)
    return (
        output.astype(BF16),
        input_grad.astype(BF16),
        both[:, 0].swapaxes(0, 1),
        both[:, 1].swapaxes(0, 1),
        grad_down.transpose(1, 2, 0),
    )


def solution(mesh):
    fine = Mesh(mesh.devices.reshape(*SIZES.values()), AXES)
    dp, shard = ("zlo", "x", "core"), ("zhi", "y")
    return jax.shard_map(
        per_device,
        mesh=fine,
        in_specs=(
            P(AXES, None),
            P(AXES, None),
            P(dp),
            P(dp),
            P(None, None, shard),
            P(None, None, shard),
            P(None, shard, None),
        ),
        out_specs=(
            P(AXES, None),
            P(AXES, None),
            P(None, dp, shard),
            P(None, dp, shard),
            P(None, shard, dp),
        ),
        check_vma=False,
    )
```

```python
import jax
import jax.numpy as jnp
from jax import lax
from jax.experimental import pallas as pl
from jax.experimental.pallas import tpu as pltpu
from jax.sharding import Mesh, PartitionSpec as P

EXP = 2
AXES = ("zlo", "x", "core", "zhi", "y")
SIZES = {"zlo": 4, "x": 4, "core": 2, "zhi": 2, "y": 4}
F32, BF16 = jnp.float32, jnp.bfloat16
TILE = 512


def send(value, axis, step):
    n = SIZES[axis]
    return lax.ppermute(value, axis, [(i, (i + step) % n) for i in range(n)])


def relative(values):
    rows = values.shape[0] // 8
    blocks = values.reshape(2, 4, rows)[:, ::-1]
    doubled = jnp.tile(blocks, (2, 2, 1))
    start = (lax.axis_index("zhi"), 3 - lax.axis_index("y"), 0)
    return lax.dynamic_slice(doubled, start, (2, 4, rows)).reshape(-1, 1)


def tie(*values):
    return lax.optimization_barrier(values)


def exchange(value, axis):
    return lax.all_to_all(value, axis, 0, 0, tiled=True)


def sends(pieces, axis, way=1):
    return [send(piece, axis, way * k) for k, piece in enumerate(pieces, 1)]


def add(own, pieces):
    for piece in pieces:
        own = own + piece.astype(F32)
    return own


def pick(value, axis):
    n = SIZES[axis]
    me = lax.axis_index(axis)
    own = lax.dynamic_index_in_dim(value, me, 0, keepdims=False)
    return own, [lax.dynamic_index_in_dim(value, (me + k) % n, 0, keepdims=False).astype(BF16) for k in range(1, n)]


def dot(a, b, ca, cb):
    return lax.dot_general(a, b, (((ca,), (cb,)), ((), ())), preferred_element_type=F32)


def split(value, second):
    zero = jnp.zeros_like(value)
    return jnp.where(second, zero, value), jnp.where(second, value, zero)


def put_rows(value, own, s1, s2, s3):
    i = pl.program_id(0)
    n = own.shape[1]
    own[pl.ds(i, 1)] = value[:n][None]
    for k, piece in enumerate((s1, s2, s3), 1):
        piece[pl.ds(i, 1)] = value[k * n : (k + 1) * n].astype(BF16)[None]


def put_grad(value, core, own, other):
    first = core == 0
    zs = own.shape[1]
    v = value.reshape(zs, 4, 2, value.shape[0] // (8 * zs), value.shape[1])
    for z in range(zs):
        own[:, z] = jnp.where(first, v[z, :, 0], v[z, :, 1]).astype(BF16)
        other[:, z] = jnp.where(first, v[z, :, 1], v[z, :, 0]).astype(BF16)


def forward_kernel(second_ref, *refs):
    blocks = refs[:8]
    wg, wu, wd, x_ref, hh_ref, a_ref, s_ref = refs[8:15]
    i = pl.program_id(0)
    n = blocks[0].shape[0]

    @pl.when(i == 0)
    def _():
        for b, block in enumerate(blocks):
            x_ref[b * n : (b + 1) * n] = block[...]

    rows = pl.ds(pl.multiple_of(i * TILE, TILE), TILE)
    second = second_ref[rows] > 0
    x0, x1 = split(x_ref[rows], second)
    xx = jnp.concatenate([x0, x1], axis=1)
    gate = dot(xx, wg[...], 1, 0)
    up = dot(xx, wu[...], 1, 0)
    sigma = 1.0 / (1.0 + jnp.exp(-gate))
    silu = gate * sigma
    a_ref[...] = up * sigma * (1.0 + gate * (1.0 - sigma))
    s_ref[...] = silu
    hidden = (silu * up).astype(BF16)
    hh = jnp.concatenate(split(hidden, second), axis=1)
    hh_ref[...] = hh
    put_rows(dot(hh, wd[...], 1, 0), *refs[15:19])


def back_kernel(second_ref, scale_ref, *refs):
    a_ref, s_ref, wd, dout, gu_ref = refs[8:]
    i = pl.program_id(0)
    n = refs[0].shape[0]

    @pl.when(i == 0)
    def _():
        for b, block in enumerate(refs[:8]):
            at = slice(b * n, (b + 1) * n)
            dout[at] = (scale_ref[at] * block[...].astype(F32)).astype(BF16)

    rows = pl.ds(pl.multiple_of(i * TILE, TILE), TILE)
    second = second_ref[...] > 0
    ff = a_ref.shape[1]
    both = dot(dout[rows], wd[...], 1, 1)
    back = jnp.where(second, both[:, ff:], both[:, :ff])
    gate_grad = (back * a_ref[...]).astype(BF16)
    up_grad = (back * s_ref[...]).astype(BF16)
    gu_ref[...] = jnp.concatenate(split(gate_grad, second) + split(up_grad, second), axis=1)


def outer_kernel(core_ref, left, right, own, other):
    put_grad(dot(left[...], right[...], 0, 0), core_ref[0], own, other)


def input_kernel(gu, wg, wu, *outs):
    ff = wg.shape[2]
    total = None
    for j, w in enumerate((wg, wu)):
        for e in range(EXP):
            c = (j * EXP + e) * ff
            term = dot(gu[:, c : c + ff], w[e], 1, 1)
            total = term if total is None else total + term
    put_rows(total, *outs)


def call(kernel, grid, ins, outs, flops, scalars=0):
    return pl.pallas_call(
        kernel,
        out_shape=[jax.ShapeDtypeStruct(a.shape, a.dtype) for *_, a in outs],
        grid_spec=pltpu.PrefetchScalarGridSpec(
            num_scalar_prefetch=scalars,
            grid=(grid,),
            in_specs=[pl.BlockSpec(b, m) for b, m, _ in ins],
            out_specs=[pl.BlockSpec(b, m) for b, m, _ in outs],
        ),
        compiler_params=pltpu.CompilerParams(vmem_limit_bytes=56 << 20),
        cost_estimate=pl.CostEstimate(flops=flops, bytes_accessed=flops // 400, transcendentals=0),
    )


def whole(a):
    return (a.shape, lambda i, *_: (0,) * len(a.shape), a)


def tiled(a, axis, size):
    block = tuple(size if d == axis else n for d, n in enumerate(a.shape))
    return (block, lambda i, *_: tuple(i if d == axis else 0 for d in range(len(a.shape))), a)


def sds(shape, dtype):
    return jax.ShapeDtypeStruct(shape, dtype)


def per_device(tokens, cotangent, assign, prob, w_gate, w_up, w_down):
    block, width = tokens.shape
    rows = assign.shape[0]
    ff = w_gate.shape[2]
    steps = rows // TILE
    own_rows = width // 32
    wide = EXP * ff
    unit = 2 * rows * width * ff * EXP
    second = relative(assign)
    scale = relative(prob)
    core = lax.axis_index("core").astype(jnp.int32).reshape(1)
    far_tokens, far_cot = send(tokens, "zhi", 1), send(cotangent, "zhi", 1)
    x0 = sends([tokens] * 3, "y")
    d0 = [send(cotangent, "y", 1)]
    far_tokens, d0[0] = tie(far_tokens, d0[0])
    d0 += [send(cotangent, "y", k) for k in (2, 3)]
    xs = [tokens, *x0, far_tokens, *sends([far_tokens] * 3, "y")]
    ds = [cotangent, *d0, far_cot, *sends([far_cot] * 3, "y")]
    wg2, wu2 = (w.reshape(EXP * width, ff) for w in (w_gate, w_up))
    wd2 = w_down.reshape(wide, width)
    pieces = [whole(sds((2, block, width), t)) for t in (F32, BF16, BF16, BF16)]

    def run(kernel, ins, outs, flops, *scalars):
        return call(kernel, steps, ins, outs, flops, len(scalars))(*scalars, *(a for *_, a in ins))

    def outer(left, right, cost):
        columns = right.shape[1]
        outs = [tiled(sds((4, 4, own_rows, columns), BF16), 1, 4 // steps)] * 2
        own, other = run(outer_kernel, [tiled(left, 1, TILE), whole(right)], outs, cost, core)
        return own, send(other, "core", 1)

    ins = [whole(a) for a in (second, *xs, wg2, wu2, wd2)]
    outs = [
        whole(sds((rows, width), BF16)),
        tiled(sds((rows, wide), BF16), 0, TILE),
        tiled(sds((rows, ff), F32), 0, TILE),
        tiled(sds((rows, ff), F32), 0, TILE),
        *pieces,
    ]
    x, hh, act, silu, out, *out_y = run(forward_kernel, ins, outs, 3 * unit)
    ds, out_y = tie(ds, out_y)
    out_y = sends(out_y, "y", -1)

    ins = [tiled(second, 0, TILE), whole(scale), *(whole(a) for a in ds)]
    ins += [tiled(act, 0, TILE), tiled(silu, 0, TILE), whole(wd2)]
    outs = [whole(sds((rows, width), BF16)), tiled(sds((rows, 2 * wide), BF16), 0, TILE)]
    dout, gu = run(back_kernel, ins, outs, unit // 20)
    both, both_c = outer(x, gu, unit // 10)
    out, out_y, both, dout = tie(out, out_y, both, dout)
    out = add(out, out_y)
    out, dout, both = tie(out, dout, both)
    far_out = send(out[1].astype(BF16), "zhi", 1)
    down, down_c = outer(dout, hh, 8 * unit)
    down, both_c, gu, both = tie(down, both_c, gu, both)
    both, both_x = pick(add(both.astype(F32), [both_c]), "x")
    gu, both, both_x = tie(gu, both, both_x)
    both_x = sends(both_x, "x")

    ins = [tiled(gu, 0, TILE), whole(w_gate), whole(w_up)]
    near, *in_y = run(input_kernel, ins, pieces, 8 * unit)
    near, in_y, down_c, far_out, both_x[0], both_x[2] = tie(near, in_y, down_c, far_out, both_x[0], both_x[2])
    in_y = sends(in_y, "y", -1)
    down, down_x = pick(add(down.astype(F32), [down_c]), "x")
    output = (out[0] + far_out.astype(F32)) * scale[:block]
    down_x = sends(down_x, "x")
    both, both_x, output, in_y[0], in_y[2], down_x[0], down_x[2] = tie(both, both_x, output, in_y[0], in_y[2], down_x[0], down_x[2])
    both = exchange(add(both, both_x).astype(BF16), "zlo")
    down, down_x, both, near, in_y[1] = tie(down, down_x, both, near, in_y[1])
    near = add(near, in_y)
    far = send(near[1].astype(BF16), "zhi", 1)
    down = exchange(add(down, down_x).astype(BF16), "zlo")
    both = add(both[0].astype(F32), both[1:]).reshape(own_rows, 2, EXP, ff)
    input_grad = near[0] + far.astype(F32)
    grad_down = add(down[0].astype(F32), down[1:]).reshape(own_rows, EXP, ff)
    return (
        output.astype(BF16),
        input_grad.astype(BF16),
        both[:, 0].swapaxes(0, 1),
        both[:, 1].swapaxes(0, 1),
        grad_down.transpose(1, 2, 0),
    )


def solution(mesh):
    fine = Mesh(mesh.devices.reshape(*SIZES.values()), AXES)
    dp, shard = ("zlo", "x", "core"), ("zhi", "y")
    return jax.shard_map(
        per_device,
        mesh=fine,
        in_specs=(
            P(AXES, None),
            P(AXES, None),
            P(dp),
            P(dp),
            P(None, None, shard),
            P(None, None, shard),
            P(None, shard, None),
        ),
        out_specs=(
            P(AXES, None),
            P(AXES, None),
            P(None, dp, shard),
            P(None, dp, shard),
            P(None, shard, dp),
        ),
        check_vma=False,
    )
```

```python
import jax
import jax.numpy as jnp
from jax import lax
from jax.experimental import pallas as pl
from jax.experimental.pallas import tpu as pltpu
from jax.sharding import Mesh, PartitionSpec as P

EXP = 2
AXES = ("zlo", "x", "core", "zhi", "y")
SIZES = {"zlo": 4, "x": 4, "core": 2, "zhi": 2, "y": 4}
F32, BF16 = jnp.float32, jnp.bfloat16
TILE = 512


def send(value, axis, step):
    n = SIZES[axis]
    return lax.ppermute(value, axis, [(i, (i + step) % n) for i in range(n)])


def relative(values):
    rows = values.shape[0] // 8
    blocks = values.reshape(2, 4, rows)[:, ::-1]
    doubled = jnp.tile(blocks, (2, 2, 1))
    start = (lax.axis_index("zhi"), 3 - lax.axis_index("y"), 0)
    return lax.dynamic_slice(doubled, start, (2, 4, rows)).reshape(-1, 1)


def tie(*values):
    return lax.optimization_barrier(values)


def exchange(value, axis):
    return lax.all_to_all(value, axis, 0, 0, tiled=True)


def sends(pieces, axis, way=1):
    return [send(piece, axis, way * k) for k, piece in enumerate(pieces, 1)]


def add(own, pieces):
    for piece in pieces:
        own = own + piece.astype(F32)
    return own


def pick(value, axis):
    n = SIZES[axis]
    me = lax.axis_index(axis)
    own = lax.dynamic_index_in_dim(value, me, 0, keepdims=False)
    return own, [lax.dynamic_index_in_dim(value, (me + k) % n, 0, keepdims=False).astype(BF16) for k in range(1, n)]


def dot(a, b, ca, cb):
    return lax.dot_general(a, b, (((ca,), (cb,)), ((), ())), preferred_element_type=F32)


def split(value, second):
    zero = jnp.zeros_like(value)
    return jnp.where(second, zero, value), jnp.where(second, value, zero)


def put_rows(value, own, s1, s2, s3):
    i = pl.program_id(0)
    n = own.shape[1]
    own[pl.ds(i, 1)] = value[:n][None]
    for k, piece in enumerate((s1, s2, s3), 1):
        piece[pl.ds(i, 1)] = value[k * n : (k + 1) * n].astype(BF16)[None]


def put_grad(value, core, own, other):
    first = core == 0
    zs = own.shape[1]
    v = value.reshape(zs, 4, 2, value.shape[0] // (8 * zs), value.shape[1])
    for z in range(zs):
        own[:, z] = jnp.where(first, v[z, :, 0], v[z, :, 1]).astype(BF16)
        other[:, z] = jnp.where(first, v[z, :, 1], v[z, :, 0]).astype(BF16)


def forward_kernel(second_ref, *refs):
    blocks = refs[:8]
    wg, wu, wd, x_ref, hh_ref, a_ref, s_ref = refs[8:15]
    i = pl.program_id(0)
    n = blocks[0].shape[0]

    @pl.when(i == 0)
    def _():
        for b, block in enumerate(blocks):
            x_ref[b * n : (b + 1) * n] = block[...]

    rows = pl.ds(pl.multiple_of(i * TILE, TILE), TILE)
    second = second_ref[rows] > 0
    x0, x1 = split(x_ref[rows], second)
    xx = jnp.concatenate([x0, x1], axis=1)
    gate = dot(xx, wg[...], 1, 0)
    up = dot(xx, wu[...], 1, 0)
    sigma = 1.0 / (1.0 + jnp.exp(-gate))
    silu = gate * sigma
    a_ref[...] = up * sigma * (1.0 + gate * (1.0 - sigma))
    s_ref[...] = silu
    hidden = (silu * up).astype(BF16)
    hh = jnp.concatenate(split(hidden, second), axis=1)
    hh_ref[...] = hh
    put_rows(dot(hh, wd[...], 1, 0), *refs[15:19])


def back_kernel(second_ref, scale_ref, *refs):
    a_ref, s_ref, wd, dout, gu_ref = refs[8:]
    i = pl.program_id(0)
    n = refs[0].shape[0]

    @pl.when(i == 0)
    def _():
        for b, block in enumerate(refs[:8]):
            at = slice(b * n, (b + 1) * n)
            dout[at] = (scale_ref[at] * block[...].astype(F32)).astype(BF16)

    rows = pl.ds(pl.multiple_of(i * TILE, TILE), TILE)
    second = second_ref[...] > 0
    ff = a_ref.shape[1]
    both = dot(dout[rows], wd[...], 1, 1)
    back = jnp.where(second, both[:, ff:], both[:, :ff])
    gate_grad = (back * a_ref[...]).astype(BF16)
    up_grad = (back * s_ref[...]).astype(BF16)
    gu_ref[...] = jnp.concatenate(split(gate_grad, second) + split(up_grad, second), axis=1)


def outer_kernel(core_ref, left, right, own, other):
    put_grad(dot(left[...], right[...], 0, 0), core_ref[0], own, other)


def input_kernel(gu, wg, wu, *outs):
    ff = wg.shape[2]
    total = None
    for j, w in enumerate((wg, wu)):
        for e in range(EXP):
            c = (j * EXP + e) * ff
            term = dot(gu[:, c : c + ff], w[e], 1, 1)
            total = term if total is None else total + term
    put_rows(total, *outs)


def call(kernel, grid, ins, outs, flops, scalars=0):
    return pl.pallas_call(
        kernel,
        out_shape=[jax.ShapeDtypeStruct(a.shape, a.dtype) for *_, a in outs],
        grid_spec=pltpu.PrefetchScalarGridSpec(
            num_scalar_prefetch=scalars,
            grid=(grid,),
            in_specs=[pl.BlockSpec(b, m) for b, m, _ in ins],
            out_specs=[pl.BlockSpec(b, m) for b, m, _ in outs],
        ),
        compiler_params=pltpu.CompilerParams(vmem_limit_bytes=56 << 20),
        cost_estimate=pl.CostEstimate(flops=flops, bytes_accessed=flops // 400, transcendentals=0),
    )


def whole(a):
    return (a.shape, lambda i, *_: (0,) * len(a.shape), a)


def tiled(a, axis, size):
    block = tuple(size if d == axis else n for d, n in enumerate(a.shape))
    return (block, lambda i, *_: tuple(i if d == axis else 0 for d in range(len(a.shape))), a)


def sds(shape, dtype):
    return jax.ShapeDtypeStruct(shape, dtype)


def per_device(tokens, cotangent, assign, prob, w_gate, w_up, w_down):
    block, width = tokens.shape
    rows = assign.shape[0]
    ff = w_gate.shape[2]
    steps = rows // TILE
    own_rows = width // 32
    wide = EXP * ff
    unit = 2 * rows * width * ff * EXP
    second = relative(assign)
    scale = relative(prob)
    core = lax.axis_index("core").astype(jnp.int32).reshape(1)
    far_tokens, far_cot = send(tokens, "zhi", 1), send(cotangent, "zhi", 1)
    x0 = sends([tokens] * 3, "y")
    d0 = [send(cotangent, "y", 1)]
    far_tokens, d0[0] = tie(far_tokens, d0[0])
    d0 += [send(cotangent, "y", k) for k in (2, 3)]
    xs = [tokens, *x0, far_tokens, *sends([far_tokens] * 3, "y")]
    ds = [cotangent, *d0, far_cot, *sends([far_cot] * 3, "y")]
    wg2, wu2 = (w.reshape(EXP * width, ff) for w in (w_gate, w_up))
    wd2 = w_down.reshape(wide, width)
    pieces = [whole(sds((2, block, width), t)) for t in (F32, BF16, BF16, BF16)]

    def run(kernel, ins, outs, flops, *scalars):
        return call(kernel, steps, ins, outs, flops, len(scalars))(*scalars, *(a for *_, a in ins))

    def outer(left, right, cost):
        columns = right.shape[1]
        outs = [tiled(sds((4, 4, own_rows, columns), BF16), 1, 4 // steps)] * 2
        own, other = run(outer_kernel, [tiled(left, 1, TILE), whole(right)], outs, cost, core)
        return own, send(other, "core", 1)

    ins = [whole(a) for a in (second, *xs, wg2, wu2, wd2)]
    outs = [
        whole(sds((rows, width), BF16)),
        tiled(sds((rows, wide), BF16), 0, TILE),
        tiled(sds((rows, ff), F32), 0, TILE),
        tiled(sds((rows, ff), F32), 0, TILE),
        *pieces,
    ]
    x, hh, act, silu, out, *out_y = run(forward_kernel, ins, outs, 3 * unit)
    ds, out_y = tie(ds, out_y)
    out_y = sends(out_y, "y", -1)

    ins = [tiled(second, 0, TILE), whole(scale), *(whole(a) for a in ds)]
    ins += [tiled(act, 0, TILE), tiled(silu, 0, TILE), whole(wd2)]
    outs = [whole(sds((rows, width), BF16)), tiled(sds((rows, 2 * wide), BF16), 0, TILE)]
    dout, gu = run(back_kernel, ins, outs, unit // 20)
    both, both_c = outer(x, gu, unit // 10)
    out, out_y, both, dout = tie(out, out_y, both, dout)
    out = add(out, out_y)
    out, dout, both = tie(out, dout, both)
    far_out = send(out[1].astype(BF16), "zhi", 1)
    down, down_c = outer(dout, hh, 8 * unit)
    down, both_c, gu, both = tie(down, both_c, gu, both)
    both, both_x = pick(add(both.astype(F32), [both_c]), "x")
    gu, both, both_x = tie(gu, both, both_x)
    both_x = sends(both_x, "x")

    ins = [tiled(gu, 0, TILE), whole(w_gate), whole(w_up)]
    near, *in_y = run(input_kernel, ins, pieces, 8 * unit)
    near, in_y, down_c, far_out, both_x[0], both_x[2] = tie(near, in_y, down_c, far_out, both_x[0], both_x[2])
    in_y = sends(in_y, "y", -1)
    down, down_x = pick(add(down.astype(F32), [down_c]), "x")
    output = (out[0] + far_out.astype(F32)) * scale[:block]
    down_x = sends(down_x, "x")
    both, both_x, output, in_y[0], in_y[2], down_x[0], down_x[2] = tie(both, both_x, output, in_y[0], in_y[2], down_x[0], down_x[2])
    both, both_z = pick(add(both, both_x), "zlo")
    both_z = sends(both_z, "zlo")
    down, down_x, both_z, near, in_y[1] = tie(down, down_x, both_z, near, in_y[1])
    near = add(near, in_y)
    far = send(near[1].astype(BF16), "zhi", 1)
    down = exchange(add(down, down_x).astype(BF16), "zlo")
    both = add(both, both_z).reshape(own_rows, 2, EXP, ff)
    input_grad = near[0] + far.astype(F32)
    grad_down = add(down[0].astype(F32), down[1:]).reshape(own_rows, EXP, ff)
    return (
        output.astype(BF16),
        input_grad.astype(BF16),
        both[:, 0].swapaxes(0, 1),
        both[:, 1].swapaxes(0, 1),
        grad_down.transpose(1, 2, 0),
    )


def solution(mesh):
    fine = Mesh(mesh.devices.reshape(*SIZES.values()), AXES)
    dp, shard = ("zlo", "x", "core"), ("zhi", "y")
    return jax.shard_map(
        per_device,
        mesh=fine,
        in_specs=(
            P(AXES, None),
            P(AXES, None),
            P(dp),
            P(dp),
            P(None, None, shard),
            P(None, None, shard),
            P(None, shard, None),
        ),
        out_specs=(
            P(AXES, None),
            P(AXES, None),
            P(None, dp, shard),
            P(None, dp, shard),
            P(None, shard, dp),
        ),
        check_vma=False,
    )
```
